32 devices in a mesh: row: 2 (over x), col: 8 (over z, y), depth: 2 (over core).
Axes of the slice: x: 2, y: 2, z: 4, core: 2. Of those that a mesh axis runs over, the one named last changes fastest.
Arguments:
- activations: bfloat16 [2, 512, 8192], P('depth', 'col', 'row'), may hold values from -6 to 6
- weight_tiles: bfloat16 [2, 8, 448, 128, 128], P('row', 'col'), may hold values from -0.09375 to 0.09375
- tile_rows: int32 [2, 8, 448], P('row', 'col'), may hold values from 0 to 31, as said below
- tile_cols: int32 [2, 8, 448], P('row', 'col'), may hold values from 0 to 27, as said below
- grad_out: bfloat16 [2, 512, 28672], P('depth', 'row', 'col'), may hold values from -6 to 6
Outputs:
- output: bfloat16 [2, 512, 28672], P('depth', 'row', 'col')
- grad_input: bfloat16 [2, 512, 8192], P('depth', 'col', 'row')
- grad_tiles: float32 [2, 8, 448, 128, 128], P('row', 'col')
The draws below stay inside these ranges and needn't reach their ends.
Inputs may be any that keep to these rules, and one draw needn't show every extreme that they name: For each block (i, j), the pairs (tile_rows[i, j, k], tile_cols[i, j, k]) over k are 448 distinct tiles of the block's 32 x 28 grid, in increasing order of tile_rows * 28 + tile_cols. `tile_cols`: drawn together with tile_rows, as stated there.
All inputs are finite; a program needn't handle non-finite values.
Results may differ from the reference program's by a relative error of at most 0.001.
Values may be sent and summed in bfloat16 or wider, within the bound.
No kernel may reach another device: no remote copies, remote signals or barrier semaphores. Data moves between devices by JAX's collectives and lax.ppermute only.
A program may use at most 256 MiB of HBM per device.

```python
import math
import jax
import jax.numpy as jnp
from jax import lax

D = 8192
FF = 28672
TILE_SIZE = 128
TOK_GROUP = 512
TILE_ROWS = 32
TILE_COLS = 28
KEPT_TILES = 448
N_ROW = 2
N_COL = 8
N_DEPTH = 2


def kept_lists(key):
    block_tiles = TILE_ROWS * TILE_COLS
    subkeys = jax.random.split(jax.random.fold_in(key, 11), N_ROW * N_COL)

    def pick_tiles(subkey):
        return jax.random.permutation(subkey, block_tiles)[:KEPT_TILES]
    chosen = jnp.sort(jax.vmap(pick_tiles)(subkeys), axis=1)
    return chosen.reshape(N_ROW, N_COL, KEPT_TILES).astype(jnp.int32)


def draw_tile_rows(key, part):
    return kept_lists(key) // TILE_COLS


def draw_tile_cols(key, part):
    return kept_lists(key) % TILE_COLS


def level_of(key, extent, pieces, smallest, top_value):
    def one(dim, parts):
        draws = jax.random.uniform(jax.random.fold_in(jax.random.fold_in(key, 6), dim), (parts,), jnp.float32, smallest / len(pieces), top_value / len(pieces))
        return jnp.repeat(jnp.exp(draws), extent[dim] // parts).reshape((-1,) + (1,) * (len(extent) - dim - 1))

    gain = one(*pieces[0])
    for cut in pieces[1:]:
        gain = gain * one(*cut)
    return gain


def normal_values(own_key, dims, width, limit, cuts=(), kind=jnp.bfloat16):
    level = level_of(own_key, dims, cuts, -0.22, 0.18) if cuts else 1.0
    drawn = jax.random.normal(own_key, dims, jnp.float32) * width * level
    return jnp.minimum(jnp.maximum(drawn, -limit), limit).astype(kind)


def setup_inputs(seed: int = 0) -> dict:
    streams_of = jax.random.split(jax.random.key(seed), 6)
    activations = normal_values(streams_of[0], (N_DEPTH, TOK_GROUP, D), 1.0, 6.0, ((0, 2), (1, 8), (2, 2)))
    weight_tiles = normal_values(streams_of[1], (N_ROW, N_COL, KEPT_TILES, TILE_SIZE, TILE_SIZE), (D // 2) ** -0.5, 0.09375, ((0, 2), (1, 8)))
    tile_rows = draw_tile_rows(jax.random.fold_in(streams_of[5], 71), 0)
    tile_cols = draw_tile_cols(jax.random.fold_in(streams_of[5], 71), 0)
    grad_out = normal_values(streams_of[4], (N_DEPTH, TOK_GROUP, FF), 1.0, 6.0, ((0, 2), (1, 2), (2, 8)))
    return {"activations": activations, "weight_tiles": weight_tiles, "tile_rows": tile_rows, "tile_cols": tile_cols, "grad_out": grad_out}


def reference(activations, weight_tiles, tile_rows, tile_cols, grad_out):
    groups = activations.shape[0]
    group_tokens = activations.shape[1]
    all_tokens = groups * group_tokens
    flat_input = activations.reshape(all_tokens, D)
    flat_grad = grad_out.reshape(all_tokens, FF)
    block_rows = D // N_ROW
    block_cols = FF // N_COL
    grad_scale = math.sqrt(all_tokens)

    def column_step(input_grad, column_index):
        grad_block = lax.dynamic_slice_in_dim(flat_grad, column_index * block_cols, block_cols, 1)
        grad_block = grad_block.astype(jnp.float32).reshape(all_tokens, TILE_COLS, TILE_SIZE)

        def row_step(carry, row_index):
            out_total, input_total = carry
            kept_weights = weight_tiles[row_index, column_index].astype(jnp.float32)
            rows_here = tile_rows[row_index, column_index]
            cols_here = tile_cols[row_index, column_index]
            input_block = lax.dynamic_slice_in_dim(flat_input, row_index * block_rows, block_rows, 1)
            input_block = input_block.astype(jnp.float32).reshape(all_tokens, TILE_ROWS, TILE_SIZE)
            input_kept = jnp.take(input_block, rows_here, axis=1)
            grad_kept = jnp.take(grad_block, cols_here, axis=1)
            forward = jnp.einsum('tkb,kbj->ktj', input_kept, kept_weights)
            forward = jax.ops.segment_sum(forward, cols_here, num_segments=TILE_COLS)
            out_total = out_total + forward.transpose(1, 0, 2).reshape(all_tokens, block_cols)
            backward = jnp.einsum('tkj,kbj->ktb', grad_kept, kept_weights)
            backward = jax.ops.segment_sum(backward, rows_here, num_segments=TILE_ROWS)
            backward = backward.transpose(1, 0, 2).reshape(all_tokens, block_rows)
            before = lax.dynamic_slice_in_dim(input_total, row_index * block_rows, block_rows, 1)
            input_total = lax.dynamic_update_slice_in_dim(input_total, before + backward, row_index * block_rows, 1)
            tile_grad = jnp.einsum('tkb,tkj->kbj', input_kept, grad_kept) / grad_scale
            return ((out_total, input_total), tile_grad)
        start_carry = (jnp.zeros((all_tokens, block_cols), jnp.float32), input_grad)
        (out_total, input_grad), tile_grads = lax.scan(row_step, start_carry, jnp.arange(N_ROW, dtype=jnp.int32))
        return (input_grad, (out_total.astype(jnp.bfloat16), tile_grads))
    input_grad, (column_outs, column_grads) = lax.scan(column_step, jnp.zeros((all_tokens, D), jnp.float32), jnp.arange(N_COL, dtype=jnp.int32))
    output = column_outs.transpose(1, 0, 2).reshape(groups, group_tokens, FF)
    grad_input = input_grad.astype(jnp.bfloat16).reshape(groups, group_tokens, D)
    grad_tiles = column_grads.transpose(1, 0, 2, 3, 4)
    return (output, grad_input, grad_tiles)
```

```python
import math

import jax
import jax.numpy as jnp
from jax import lax
from jax.experimental import pallas as pl
from jax.experimental.pallas import tpu as pltpu
from jax.sharding import PartitionSpec as P


TILE = 128
GROUP = 2 * TILE
LANES = 128
CHUNK = 32
OUT_CHUNK = 16
LEVELS = 32600.0
SMALL = 1e-30
VMEM_LIMIT = 56 * 1024 * 1024


def params(limit=VMEM_LIMIT):
    return pltpu.CompilerParams(vmem_limit_bytes=limit)


def encode(values):
    top = jnp.maximum(jnp.max(jnp.abs(values), axis=1, keepdims=True), SMALL)
    eighths = jnp.ceil(8.0 * jnp.log2(top * (1.0 / LEVELS)))
    codes = jnp.round(values * jnp.exp2(eighths * -0.125)).astype(jnp.int32).astype(jnp.int16)
    return codes, eighths


def decode(codes, eighths):
    return codes.astype(jnp.int32).astype(jnp.float32) * jnp.exp2(eighths * 0.125)


def lane_of(shape):
    return lax.broadcasted_iota(jnp.int32, shape, len(shape) - 1)


def pick_lane(values, lane):
    values = values.astype(jnp.int32).astype(jnp.float32)
    return jnp.sum(jnp.where(lane_of(values.shape) == lane, values, 0.0), axis=1, keepdims=True)


def put_lane(values, column, lane):
    return jnp.where(lane_of(values.shape) == lane, column, values)


def pack(values):
    return values.astype(jnp.int32).astype(jnp.int16)


def strip_matmul(blocks, order, weight, count_rows, count_cols, along_rows, coded, kept, gathered, instead=None):
    builds = isinstance(weight, tuple)
    outer_tiles = count_rows if along_rows else count_cols
    width = GROUP * 2 if outer_tiles % 4 == 0 else GROUP
    per = width // TILE
    steps = outer_tiles // per
    inner = (count_cols if along_rows else count_rows) * TILE
    outer = outer_tiles * TILE
    tokens = sum(rows for _, rows, _ in blocks)
    first_kept = tokens - kept
    strip_shape = (width, inner) if along_rows else (inner, width)
    spots = 0
    meta = order
    if builds:
        tiles, places, ends = weight
        kept_tiles = tiles.shape[0]
        chunk = CHUNK if kept_tiles % CHUNK == 0 else kept_tiles
        chunks = kept_tiles // chunk
        ends = (ends[per - 1 :: per] + (chunk - 1)) // chunk
        meta = jnp.concatenate([places.reshape(-1), jnp.zeros((1,), jnp.int32), ends, order])
        spots = count_rows * count_cols + 1 + steps

    def kernel(meta, *refs):
        ins, refs = refs[: len(blocks)], refs[len(blocks) :]
        weight_ref, refs = refs[0], refs[1:]
        if instead:
            instead_ref, refs = refs[0], refs[1:]
        if coded:
            codes_ref, refs = refs[0], refs[1:]
        if kept:
            kept_ref, refs = refs[0], refs[1:]
        if gathered:
            gathered_ref, refs = refs[0], refs[1:]
        if builds:
            built_ref, refs = refs[0], refs[1:]
        held, refs = refs[0], refs[1:]
        step = pl.program_id(0)

        @pl.when(step == 0)
        def _():
            held[...] = jnp.zeros_like(held)

        def mixed(here, there):
            rows = coded // len(instead[2])
            out = []
            for (a, n), (b, m) in instead[2]:
                one, two = (v[i * rows : (i + 1) * rows] for v, i in (((here, there)[a], n), ((here, there)[b], m)))
                out.append(jnp.where(meta[spots + instead[1]] == 1, one, two))
            return jnp.concatenate(out, axis=0)

        if builds:
            local, sems = refs

            def chunk_copy(n):
                here = pl.ds(n * chunk, chunk)
                return pltpu.make_async_copy(weight_ref.at[here], local.at[here], sems.at[n])

            @pl.when(step == 0)
            def _():
                for n in range(chunks):
                    chunk_copy(n).start()
                local[kept_tiles] = jnp.zeros((TILE, TILE), jnp.bfloat16)

            base = count_rows * count_cols
            lax.fori_loop(meta[base + step], meta[base + step + 1], lambda n, c: (chunk_copy(n).wait(), c)[1], 0)

            @pl.when(step == steps - 1)
            def _():
                lax.fori_loop(meta[base + step + 1], chunks, lambda n, c: (chunk_copy(n).wait(), c)[1], 0)

            for a in range(per):
                for c in range(count_cols):
                    tile = meta[(step * per + a) * count_cols + c]
                    built_ref[a * TILE : (a + 1) * TILE, c * TILE : (c + 1) * TILE] = local[tile]
            strip = built_ref[...]
        else:
            strip = weight_ref[...]
        x = jnp.concatenate([r[...] for r in ins], axis=0) if len(ins) > 1 else ins[0][...]
        if along_rows:
            y = lax.dot_general(x, strip, (((1,), (1,)), ((), ())), preferred_element_type=jnp.float32)
        else:
            y = jnp.dot(x, strip, preferred_element_type=jnp.float32)
        if coded:
            for g in range(width // GROUP):
                codes, eighths = encode(y[:coded, g * GROUP : (g + 1) * GROUP])
                here = pl.ds(pl.multiple_of(step * width + g * GROUP, GROUP), GROUP)
                if instead:
                    codes = mixed(codes, instead_ref[:, here])
                codes_ref[:, here] = codes
                held[...] = put_lane(held[...], eighths, step * (width // GROUP) + g)

            @pl.when(step == steps - 1)
            def _():
                last = pack(held[...])
                if instead:
                    last = mixed(last, instead_ref[:, outer:])
                codes_ref[:, outer:] = last

        if kept:
            kept_ref[...] = y[first_kept:]
        if gathered:

            @pl.when(step == 0)
            def _():
                gathered_ref[...] = x

    def in_spec(rows, entry):
        def place(step, meta):
            return (0 if entry is None else meta[spots + entry], 0)

        return pl.BlockSpec((rows, inner), place, pipeline_mode=pl.Buffered(1))

    outs, out_specs = [], []
    if coded:
        outs.append(jax.ShapeDtypeStruct((coded, outer + LANES), jnp.int16))
        out_specs.append(pl.BlockSpec((coded, outer + LANES), lambda s, m: (0, 0)))
    if kept:
        outs.append(jax.ShapeDtypeStruct((kept, outer), jnp.float32))
        out_specs.append(pl.BlockSpec((kept, width), lambda s, m: (0, s)))
    if gathered:
        outs.append(jax.ShapeDtypeStruct((tokens, inner), jnp.bfloat16))
        out_specs.append(pl.BlockSpec((tokens, inner), lambda s, m: (0, 0)))
    scratch = [pltpu.VMEM((max(coded, 8), LANES), jnp.float32)]
    strip_spec = pl.BlockSpec(strip_shape, (lambda s, m: (s, 0)) if along_rows else (lambda s, m: (0, s)))
    if builds:
        outs.append(jax.ShapeDtypeStruct((count_rows * TILE, count_cols * TILE), jnp.bfloat16))
        out_specs.append(strip_spec)
        strip_spec = pl.BlockSpec(memory_space=pl.ANY)
        scratch += [pltpu.VMEM((kept_tiles + 1, TILE, TILE), jnp.bfloat16), pltpu.SemaphoreType.DMA((chunks,))]
    return pl.pallas_call(
        kernel,
        out_shape=outs,
        grid_spec=pltpu.PrefetchScalarGridSpec(
            num_scalar_prefetch=1,
            grid=(steps,),
            in_specs=[in_spec(rows, entry) for _, rows, entry in blocks]
            + [strip_spec]
            + ([pl.BlockSpec((coded, outer + LANES), lambda s, m: (0, 0), pipeline_mode=pl.Buffered(1))] * bool(instead)),
            out_specs=out_specs,
            scratch_shapes=scratch,
        ),
        compiler_params=params(),
        cost_estimate=pl.CostEstimate(
            flops=2 * tokens * inner * outer,
            bytes_accessed=inner * outer * 2 + tokens * (inner * 2 + outer * 4),
            transcendentals=0,
        ),
        name="dgrad" if along_rows else "forward",
    )(meta, *[a for a, _, _ in blocks], tiles if builds else weight, *([instead[0]] if instead else []))


def tile_products(lefts, rights, order, places, ends, kept_tiles, count_rows, count_cols, factor, part, before):
    tokens = sum(rows * len(entries) for _, rows, entries in lefts)
    first, count = part
    wide_rows, wide_cols = count * TILE, count_cols * TILE
    per = 4 if count % 4 == 0 else 2
    cols_per = 4 if count_cols % 4 == 0 else 2
    row_steps, col_steps = count // per, count_cols // cols_per
    spots = count_rows * count_cols
    meta = jnp.concatenate([places.reshape(-1), jnp.zeros((1,), jnp.int32), ends, order])
    copies = sum(len(e) for _, _, e in lefts) + sum(len(e) for _, _, e in rights)

    def kernel(meta, *refs):
        left_refs, refs = refs[: len(lefts)], refs[len(lefts) :]
        right_refs, refs = refs[: len(rights)], refs[len(rights) :]
        if before is not None:
            refs = refs[1:]
        out_ref, left_all, right_all, turned, found, in_sems, out_sems = refs
        i, j = pl.program_id(0), pl.program_id(1)

        def input_copies():
            n = 0
            for group, group_refs, whole, cols in (
                (lefts, left_refs, left_all, pl.ds(first * TILE, wide_rows)),
                (rights, right_refs, right_all, pl.ds(0, wide_cols)),
            ):
                for (_, rows, entries), ref in zip(group, group_refs):
                    for b, entry in enumerate(entries):
                        to = pl.multiple_of(meta[spots + 1 + count_rows + entry] * rows, rows)
                        yield pltpu.make_async_copy(
                            ref.at[pl.ds(b * rows, rows), cols], whole.at[pl.ds(to, rows), :], in_sems.at[n]
                        )
                        n += 1

        @pl.when((i == 0) & (j == 0))
        def _():
            for c in input_copies():
                c.start()
            for c in input_copies():
                c.wait()
            turned[0] = left_all[:, : per * TILE].T

        now = lax.rem(i, 2)
        cols = pl.ds(pl.multiple_of(j * cols_per * TILE, cols_per * TILE), cols_per * TILE)
        sums = jnp.dot(turned[now], right_all[:, cols], preferred_element_type=jnp.float32) * factor
        for a in range(per):
            for b in range(cols_per):
                tile = meta[(first + i * per + a) * count_cols + j * cols_per + b]
                found[tile] = sums[a * TILE : (a + 1) * TILE, b * TILE : (b + 1) * TILE]
        piece = lax.rem(j, per)
        ahead = jnp.minimum(i + 1, row_steps - 1) * per + piece
        turned[1 - now, pl.ds(pl.multiple_of(piece * TILE, TILE), TILE), :] = left_all[
            :, pl.ds(pl.multiple_of(ahead * TILE, TILE), TILE)
        ].T

        def out_copies(low, high, begin):
            many = (high - low) // OUT_CHUNK

            def copy(at, size, sem):
                c = pltpu.make_async_copy(found.at[pl.ds(at, size)], out_ref.at[pl.ds(at, size)], sem)
                c.start() if begin else c.wait()

            def chunk(n, c):
                copy(low + n * OUT_CHUNK, OUT_CHUNK, out_sems.at[0])
                return c

            def single(n, c):
                copy(n, 1, out_sems.at[1])
                return c

            lax.fori_loop(0, many, chunk, 0)
            lax.fori_loop(low + many * OUT_CHUNK, high, single, 0)

        def bounds(n):
            row = spots + first + n * per
            return meta[row], meta[row + per]

        @pl.when(j == col_steps - 1)
        def _():
            out_copies(*bounds(i), True)

        @pl.when((i == row_steps - 1) & (j == col_steps - 1))
        def _():
            for n in range(row_steps):
                out_copies(*bounds(n), False)

    operands = [a for a, _, _ in lefts] + [a for a, _, _ in rights]
    aliases = {}
    if before is not None:
        aliases = {1 + len(operands): 0}
        operands.append(before)
    return pl.pallas_call(
        kernel,
        out_shape=jax.ShapeDtypeStruct((kept_tiles, TILE, TILE), jnp.float32),
        grid_spec=pltpu.PrefetchScalarGridSpec(
            num_scalar_prefetch=1,
            grid=(row_steps, col_steps),
            in_specs=[pl.BlockSpec(memory_space=pl.ANY)] * len(operands),
            out_specs=pl.BlockSpec(memory_space=pl.ANY),
            scratch_shapes=[
                pltpu.VMEM((tokens, wide_rows), jnp.bfloat16),
                pltpu.VMEM((tokens, wide_cols), jnp.bfloat16),
                pltpu.VMEM((2, per * TILE, tokens), jnp.bfloat16),
                pltpu.VMEM((kept_tiles + 1, TILE, TILE), jnp.float32),
                pltpu.SemaphoreType.DMA((copies,)),
                pltpu.SemaphoreType.DMA((2,)),
            ],
        ),
        input_output_aliases=aliases,
        compiler_params=params(),
        cost_estimate=pl.CostEstimate(
            flops=2 * tokens * wide_rows * wide_cols,
            bytes_accessed=tokens * (wide_rows + wide_cols) * 2
            + kept_tiles * TILE * TILE * 4 * count // count_rows,
            transcendentals=0,
        ),
        name="wgrad",
    )(meta, *operands)


def add_received(terms, order, rows, wide, sends, keeps, keep_type):
    span = 1024 if wide % 1024 == 0 else wide
    steps, groups = wide // span, span // GROUP

    def kernel(meta, *refs):
        ins, refs = refs[: 3 * len(terms)], refs[3 * len(terms) :]
        if sends:
            codes_ref, refs = refs[0], refs[1:]
        keep_ref, held = refs
        step = pl.program_id(0)

        @pl.when(step == 0)
        def _():
            held[...] = jnp.zeros_like(held)

        for g in range(groups):
            here = slice(g * GROUP, (g + 1) * GROUP)
            there = pl.ds(pl.multiple_of(step * span + g * GROUP, GROUP), GROUP)
            sums = []
            for p in range(len(terms)):
                local, codes, last = ins[3 * p : 3 * p + 3]
                eighths = pick_lane(last[...], step * groups + g)
                sums.append(local[:, here] + decode(codes[:, here], eighths))
            for n, keep in enumerate(keeps):
                keep_ref[n * rows : (n + 1) * rows, here] = keep(sums, meta).astype(keep_type)
            for n, send in enumerate(sends):
                codes, eighths = encode(send(sums, meta))
                codes_ref[n * rows : (n + 1) * rows, there] = codes
                held[n] = put_lane(held[n], eighths, step * groups + g)

        @pl.when(step == steps - 1)
        def _():
            for n in range(len(sends)):
                codes_ref[n * rows : (n + 1) * rows, wide:] = pack(held[n])

    in_specs, operands = [], []
    for local, local_entry, codes, entry in terms:
        in_specs += [
            pl.BlockSpec((rows, span), lambda s, m, e=local_entry: (m[e], s)),
            pl.BlockSpec((rows, span), lambda s, m, e=entry: (m[e], s)),
            pl.BlockSpec((rows, LANES), lambda s, m, e=entry: (m[e], wide // LANES)),
        ]
        operands += [local, codes, codes]
    outs, out_specs = [], []
    if sends:
        outs.append(jax.ShapeDtypeStruct((len(sends) * rows, wide + LANES), jnp.int16))
        out_specs.append(pl.BlockSpec((len(sends) * rows, wide + LANES), lambda s, m: (0, 0)))
    outs.append(jax.ShapeDtypeStruct((len(keeps) * rows, wide), keep_type))
    out_specs.append(pl.BlockSpec((len(keeps) * rows, span), lambda s, m: (0, s)))
    return pl.pallas_call(
        kernel,
        out_shape=outs,
        grid_spec=pltpu.PrefetchScalarGridSpec(
            num_scalar_prefetch=1,
            grid=(steps,),
            in_specs=in_specs,
            out_specs=out_specs,
            scratch_shapes=[pltpu.VMEM((max(len(sends), 1), rows, LANES), jnp.float32)],
        ),
        compiler_params=params(),
        cost_estimate=pl.CostEstimate(
            flops=8 * rows * wide, bytes_accessed=len(terms) * rows * wide * 10, transcendentals=0
        ),
        name="add_received",
    )(order, *operands)


def tile_places(tile_rows, tile_cols, count_rows, count_cols):
    kept = tile_rows.shape[0]
    position = tile_rows * count_cols + tile_cols
    short = jnp.arange(kept, dtype=jnp.int32) - kept
    spot = jnp.arange(count_rows * count_cols, dtype=jnp.int32)
    places = jnp.sum(jnp.where(position[None, :] == spot[:, None], short[None, :], 0), axis=1) + kept
    rows = jnp.arange(count_rows, dtype=jnp.int32)
    ends = jnp.sum((tile_rows[None, :] <= rows[:, None]).astype(jnp.int32), axis=1)
    return places, ends


def shards_general(activations, weight_tiles, tile_rows, tile_cols, grad_out):
    tiles = weight_tiles[0, 0]
    count_rows = activations.shape[2] // TILE
    count_cols = grad_out.shape[2] // TILE
    places, ends = tile_places(tile_rows[0, 0], tile_cols[0, 0], count_rows, count_cols)
    none = jnp.arange(2, dtype=jnp.int32)
    act = lax.all_gather(activations[0], "col", axis=0, tiled=True)
    grad = lax.all_gather(grad_out[0], "row", axis=0, tiled=True)
    tokens = act.shape[0]
    build = (tiles, places, ends)
    back, weight = strip_matmul([(grad, tokens, None)], none, build, count_rows, count_cols, True, 0, tokens, False)
    (partial,) = strip_matmul([(act, tokens, None)], none, weight, count_rows, count_cols, False, 0, tokens, False)
    output = lax.psum_scatter(partial, "row", scatter_dimension=0, tiled=True).astype(jnp.bfloat16)[None]
    grad_input = lax.psum_scatter(back, "col", scatter_dimension=0, tiled=True).astype(jnp.bfloat16)[None]
    groups = lax.axis_size("depth")
    all_act = lax.all_gather(act, "depth", axis=0, tiled=True)
    all_grad = lax.all_gather(grad, "depth", axis=0, tiled=True)
    grad_tiles = tile_products(
        [(all_act, tokens * groups, [0])],
        [(all_grad, tokens * groups, [0])],
        none,
        places,
        ends,
        tiles.shape[0],
        count_rows,
        count_cols,
        1.0 / math.sqrt(tokens * groups),
        (0, count_rows),
        None,
    )
    return output, grad_input, grad_tiles[None, None]


def swap(value, axis, bit, size):
    return lax.ppermute(value, axis, [(i, i ^ bit) for i in range(size)])


def shards_paired(activations, weight_tiles, tile_rows, tile_cols, grad_out):
    tiles = weight_tiles[0, 0]
    count_rows = activations.shape[2] // TILE
    count_cols = grad_out.shape[2] // TILE
    wide_rows = activations.shape[2]
    size = lax.axis_size("col")
    row, col = lax.axis_index("row"), lax.axis_index("col")
    y, z0, z1 = col % 2, col // 2 % 2, col // 4
    block = activations.shape[1]
    half = grad_out.shape[1]
    places, ends = tile_places(tile_rows[0, 0], tile_cols[0, 0], count_rows, count_cols)

    def swap_col(value, bit):
        return swap(value, "col", bit, size)

    def swap_depth(value):
        return swap(value, "depth", 1, 2)

    def swap_row(value):
        return swap(value, "row", 1, 2)

    grad_mine = grad_out[0]
    own = activations[0]
    grad_other = swap_row(grad_mine)
    b2 = swap_col(own, 2)
    b6 = swap_col(own, 6)
    b1 = swap_col(own, 1)
    b3 = swap_col(b2, 1)
    b4 = swap_col(b6, 2)
    b7 = swap_col(b6, 1)
    b5 = swap_col(b4, 1)
    send_near = (z1 != row).astype(jnp.int32)

    def dgrad(grad, weight):
        blocks = [(grad, block, e) for e in range(4)]
        order = jnp.stack([1 - y, 3 - y, y, 2 + y]).astype(jnp.int32)
        return strip_matmul(blocks, order, weight, count_rows, count_cols, True, 2 * block, 2 * block, False)

    def forward(blocks, weight, instead):
        blocks = [(b, block, None) for b in blocks]
        order = send_near[None]
        return strip_matmul(blocks, order, weight, count_rows, count_cols, False, half, half, True, instead)

    first_set, second_set = (0, 1, 2, 6), (3, 4, 5, 7)
    codes_mine, kept_mine, weight = dgrad(grad_mine, (tiles, places, ends))
    codes_mine = swap_col(codes_mine, 1)
    first_codes, first_kept, first_act = forward([own, b1, b2, b6], weight, None)
    codes_other, kept_other = dgrad(grad_other, weight)
    codes_other = swap_col(codes_other, 1)
    pairs = []
    for n in range(4):
        pairs.append(
            tuple((1, first_set.index(k)) if k in first_set else (0, second_set.index(k)) for k in (n, n + 4))
        )
    out_codes, second_kept, second_act = forward([b3, b4, b5, b7], weight, (first_codes, 0, pairs))
    out_codes = swap_row(out_codes)

    order = jnp.stack([z0, 1 - z0, (z1 == row).astype(jnp.int32), 0 * z0, 0 * z0 + 1]).astype(jnp.int32)
    terms = [
        (kept, e, codes, e) for kept, codes in ((kept_mine, codes_mine), (kept_other, codes_other)) for e in (0, 1)
    ]
    codes, kept = add_received(
        terms,
        order,
        block,
        wide_rows,
        [lambda s, m: s[1], lambda s, m: s[3]],
        [lambda s, m: s[0], lambda s, m: s[2]],
        jnp.float32,
    )
    codes = swap_col(codes, 2)

    groups = lax.axis_size("depth")
    partner = [swap_depth(v) for v in (first_act, second_act, grad_mine, grad_other)]
    places_order = [g * size + (col ^ k) for g in range(groups) for k in first_set + second_set]
    places_order += [2 * g + (row if k == 0 else 1 - row) for g in range(groups) for k in range(2)]
    places_order = jnp.stack(places_order).astype(jnp.int32)
    lefts = [(v, block, [4 * n + k for k in range(4)]) for n, v in enumerate((first_act, second_act, *partner[:2]))]
    rights = [(v, half, [groups * size + n]) for n, v in enumerate((grad_mine, grad_other, *partner[2:]))]

    def wgrad(part, before):
        return tile_products(
            lefts,
            rights,
            places_order,
            places,
            ends,
            tiles.shape[0],
            count_rows,
            count_cols,
            1.0 / math.sqrt(size * block * groups),
            part,
            before,
        )

    middle = count_rows // 2
    grad_tiles = wgrad((0, middle), None)
    terms = [(kept, 3, codes, 3), (kept, 4, codes, 4)]
    codes, kept = add_received(
        terms,
        order,
        block,
        wide_rows,
        [lambda s, m: jnp.where(m[2] == 1, s[1], s[0])],
        [lambda s, m: jnp.where(m[2] == 1, s[0], s[1])],
        jnp.float32,
    )
    codes = swap_col(codes, 4)
    grad_tiles = wgrad((middle, count_rows - middle), grad_tiles)
    (grad_input,) = add_received([(kept, 3, codes, 3)], order, block, wide_rows, [], [lambda s, m: s[0]], jnp.bfloat16)
    output = join_output(first_kept, second_kept, pairs, out_codes, send_near, col, block)
    return output[None], grad_input[None], grad_tiles[None, None]


def join_output(first, second, pairs, codes, send_near, col, rows):
    wide = first.shape[1]
    blocks = first.shape[0] // rows
    order = jnp.arange(blocks, dtype=jnp.int32) ^ (col % blocks)
    table = jnp.array([[[1 - p[w][0] for p in pairs], [p[w][1] for p in pairs]] for w in (0, 1)], jnp.int32)
    table = jnp.where(send_near == 1, table[1], table[0])
    chosen, index = (jnp.sum(jnp.where(order[:, None] == jnp.arange(blocks), t[None], 0), axis=1) for t in table)
    meta = jnp.concatenate([order, chosen, jnp.where(chosen == 1, 0, index), jnp.where(chosen == 1, index, 0)])
    meta = meta.astype(jnp.int32)

    def kernel(meta, first_ref, second_ref, codes_ref, out_ref):
        use_second = meta[blocks + pl.program_id(0)] == 1
        for g in range(wide // GROUP):
            here = slice(g * GROUP, (g + 1) * GROUP)
            local = jnp.where(use_second, second_ref[:, here], first_ref[:, here])
            eighths = pick_lane(codes_ref[:, wide:], g)
            out_ref[:, here] = (local + decode(codes_ref[:, here], eighths)).astype(jnp.bfloat16)

    return pl.pallas_call(
        kernel,
        out_shape=jax.ShapeDtypeStruct((blocks * rows, wide), jnp.bfloat16),
        grid_spec=pltpu.PrefetchScalarGridSpec(
            num_scalar_prefetch=1,
            grid=(blocks,),
            in_specs=[
                pl.BlockSpec((rows, wide), lambda n, m: (m[2 * blocks + n], 0)),
                pl.BlockSpec((rows, wide), lambda n, m: (m[3 * blocks + n], 0)),
                pl.BlockSpec((rows, wide + LANES), lambda n, m: (m[n], 0)),
            ],
            out_specs=pl.BlockSpec((rows, wide), lambda n, m: (n, 0)),
        ),
        compiler_params=params(),
        cost_estimate=pl.CostEstimate(flops=8 * first.size, bytes_accessed=first.size * 8, transcendentals=0),
        name="join_output",
    )(meta, first, second, codes)


def solution(mesh):
    specs = (
        P("depth", "col", "row"),
        P("row", "col", None, None, None),
        P("row", "col", None),
        P("row", "col", None),
        P("depth", "row", "col"),
    )
    paired = mesh.shape["row"] == 2 and mesh.shape["col"] == 8 and mesh.shape["depth"] == 2

    def body(*args):
        return (shards_paired if paired else shards_general)(*args)

    return jax.shard_map(
        body,
        mesh=mesh,
        in_specs=specs,
        out_specs=(specs[4], specs[0], specs[1]),
        check_vma=False,
    )
```

```python
import math

import jax
import jax.numpy as jnp
import numpy as np
from jax import lax
from jax.experimental import pallas as pl
from jax.experimental.pallas import tpu as pltpu
from jax.sharding import PartitionSpec as P


TILE = 128
GROUP = 2 * TILE
LANES = 128
WHOLE = 12582912.0
CHUNK = 32
OUT_CHUNK = 16
LEVELS = 32600.0
SMALL = 1e-30
VMEM_LIMIT = 63 * 1024 * 1024


def params(limit=VMEM_LIMIT):
    return pltpu.CompilerParams(vmem_limit_bytes=limit)


def encode(values):
    top = jnp.maximum(jnp.max(jnp.abs(values), axis=1, keepdims=True), SMALL)
    eighths = jnp.ceil(8.0 * jnp.log2(top * (1.0 / LEVELS)))
    codes = (values * jnp.exp2(eighths * -0.125) + WHOLE) - WHOLE
    return pack(codes), eighths


def decode(codes, eighths):
    return codes.astype(jnp.int32).astype(jnp.float32) * jnp.exp2(eighths * 0.125)


def lane_of(shape):
    return lax.broadcasted_iota(jnp.int32, shape, len(shape) - 1)


def pick_lane(values, lane):
    values = values.astype(jnp.int32).astype(jnp.float32)
    return jnp.sum(jnp.where(lane_of(values.shape) == lane, values, 0.0), axis=1, keepdims=True)


def put_lane(values, column, lane):
    return jnp.where(lane_of(values.shape) == lane, column, values)


def pack(values):
    return values.astype(jnp.int32).astype(jnp.int16)


def strip_matmul(blocks, meta, weight, count_rows, count_cols, along_rows, coded, kept, gathered, instead=None):
    builds = isinstance(weight, tuple)
    outer_tiles = count_rows if along_rows else count_cols
    width = next(w for w in (GROUP * 4, GROUP * 2, GROUP) if outer_tiles * TILE % w == 0)
    if not along_rows or isinstance(weight, tuple):
        width = min(width, GROUP * 2)
    per = width // TILE
    steps = outer_tiles // per
    inner = (count_cols if along_rows else count_rows) * TILE
    outer = outer_tiles * TILE
    tokens = sum(rows for _, rows, _ in blocks)
    first_kept = tokens - kept
    strip_shape = (width, inner) if along_rows else (inner, width)
    if builds:
        (tiles,) = weight
        kept_tiles = tiles.shape[0]
        chunk = CHUNK if kept_tiles % CHUNK == 0 else kept_tiles
        chunks = kept_tiles // chunk

    def kernel(meta, *refs):
        ins, refs = refs[: len(blocks)], refs[len(blocks) :]
        weight_ref, refs = refs[0], refs[1:]
        if instead:
            instead_ref, refs = refs[0], refs[1:]
        if coded:
            codes_ref, refs = refs[0], refs[1:]
        if kept:
            kept_ref, refs = refs[0], refs[1:]
        if gathered:
            gathered_ref, refs = refs[0], refs[1:]
        if builds:
            built_ref, refs = refs[0], refs[1:]
        held, refs = refs[0], refs[1:]
        step = pl.program_id(0)

        @pl.when(step == 0)
        def _():
            held[...] = jnp.zeros_like(held)

        def mixed(here, there):
            rows = coded // len(instead[2])
            out = []
            for (a, n), (b, m) in instead[2]:
                one, two = (v[i * rows : (i + 1) * rows] for v, i in (((here, there)[a], n), ((here, there)[b], m)))
                out.append(jnp.where(meta[instead[1]] == 1, one, two))
            return jnp.concatenate(out, axis=0)

        if builds:
            local, sems = refs

            def chunk_copy(n):
                here = pl.ds(n * chunk, chunk)
                return pltpu.make_async_copy(weight_ref.at[here], local.at[here], sems.at[n])

            @pl.when(step == 0)
            def _():
                for n in range(chunks):
                    chunk_copy(n).start()
                local[kept_tiles] = jnp.zeros((TILE, TILE), jnp.bfloat16)

            base = count_rows * count_cols
            held_chunks = (meta[base + step * per] + (chunk - 1)) // chunk
            needed = jnp.where(step == steps - 1, chunks, (meta[base + step * per + per] + (chunk - 1)) // chunk)
            lax.fori_loop(held_chunks, needed, lambda n, c: (chunk_copy(n).wait(), c)[1], 0)

            for a in range(per):
                for c in range(count_cols):
                    tile = meta[(step * per + a) * count_cols + c]
                    built_ref[a * TILE : (a + 1) * TILE, c * TILE : (c + 1) * TILE] = local[tile]
            strip = built_ref[...]
        else:
            strip = weight_ref[...]
        x = jnp.concatenate([r[...] for r in ins], axis=0) if len(ins) > 1 else ins[0][...]
        if along_rows:
            y = lax.dot_general(x, strip, (((1,), (1,)), ((), ())), preferred_element_type=jnp.float32)
        else:
            y = jnp.dot(x, strip, preferred_element_type=jnp.float32)
        if coded:
            for g in range(width // GROUP):
                codes, eighths = encode(y[:coded, g * GROUP : (g + 1) * GROUP])
                here = pl.ds(pl.multiple_of(step * width + g * GROUP, GROUP), GROUP)
                if instead:
                    codes = mixed(codes, instead_ref[:, here])
                codes_ref[:, here] = codes
                held[...] = put_lane(held[...], eighths, step * (width // GROUP) + g)

            @pl.when(step == steps - 1)
            def _():
                last = pack(held[...])
                if instead:
                    last = mixed(last, instead_ref[:, outer:])
                codes_ref[:, outer:] = last

        if kept:
            kept_ref[...] = y[first_kept:]
        if gathered:

            @pl.when(step == 0)
            def _():
                gathered_ref[...] = x

    def in_spec(rows, entry):
        def place(step, meta):
            return (0 if entry is None else meta[entry], 0)

        return pl.BlockSpec((rows, inner), place, pipeline_mode=pl.Buffered(1))

    outs, out_specs = [], []
    if coded:
        outs.append(jax.ShapeDtypeStruct((coded, outer + LANES), jnp.int16))
        out_specs.append(pl.BlockSpec((coded, outer + LANES), lambda s, m: (0, 0)))
    if kept:
        outs.append(jax.ShapeDtypeStruct((kept, outer), jnp.float32))
        out_specs.append(pl.BlockSpec((kept, width), lambda s, m: (0, s)))
    if gathered:
        outs.append(jax.ShapeDtypeStruct((tokens, inner), jnp.bfloat16))
        out_specs.append(pl.BlockSpec((tokens, inner), lambda s, m: (0, 0)))
    scratch = [pltpu.VMEM((max(coded, 8), LANES), jnp.float32)]
    strip_spec = pl.BlockSpec(strip_shape, (lambda s, m: (s, 0)) if along_rows else (lambda s, m: (0, s)))
    if builds:
        outs.append(jax.ShapeDtypeStruct((count_rows * TILE, count_cols * TILE), jnp.bfloat16))
        out_specs.append(strip_spec)
        strip_spec = pl.BlockSpec(memory_space=pl.ANY)
        scratch += [pltpu.VMEM((kept_tiles + 1, TILE, TILE), jnp.bfloat16), pltpu.SemaphoreType.DMA((chunks,))]
    return pl.pallas_call(
        kernel,
        out_shape=outs,
        grid_spec=pltpu.PrefetchScalarGridSpec(
            num_scalar_prefetch=1,
            grid=(steps,),
            in_specs=[in_spec(rows, entry) for _, rows, entry in blocks]
            + [strip_spec]
            + ([pl.BlockSpec((coded, outer + LANES), lambda s, m: (0, 0), pipeline_mode=pl.Buffered(1))] * bool(instead)),
            out_specs=out_specs,
            scratch_shapes=scratch,
        ),
        compiler_params=params(),
        cost_estimate=pl.CostEstimate(
            flops=2 * tokens * inner * outer,
            bytes_accessed=inner * outer * 2 + tokens * (inner * 2 + outer * 4),
            transcendentals=0,
        ),
        name="dgrad" if along_rows else "forward",
    )(meta, *[a for a, _, _ in blocks], tiles if builds else weight, *([instead[0]] if instead else []))


def tile_products(lefts, rights, meta, kept_tiles, count_rows, count_cols, factor, part, before):
    tokens = sum(rows * len(entries) for _, rows, entries in lefts)
    first, count = part
    wide_rows, wide_cols = count * TILE, count_cols * TILE
    per = next(p for p in (8, 4, 2, 1) if count % p == 0)
    steps = count // per
    spots = count_rows * count_cols

    def kernel(meta, *refs):
        left_refs, refs = refs[: len(lefts)], refs[len(lefts) :]
        right_refs, refs = refs[: len(rights)], refs[len(rights) :]
        if before is not None:
            refs = refs[1:]
        out_ref, left_all, right_all, turned, found, left_sems, right_sems, out_sems = refs
        i = pl.program_id(0)

        def copies(group, group_refs, whole, sems, from_col, to_col, width):
            n = 0
            for (_, rows, entries), ref in zip(group, group_refs):
                for b, entry in enumerate(entries):
                    to = pl.multiple_of(meta[entry] * rows, rows)
                    yield pltpu.make_async_copy(
                        ref.at[pl.ds(b * rows, rows), pl.ds(from_col, width)],
                        whole.at[pl.ds(to, rows), pl.ds(to_col, width)],
                        sems.at[n],
                    )
                    n += 1

        def left_copies(step):
            at = step * per * TILE
            return copies(lefts, left_refs, left_all, left_sems.at[step], first * TILE + at, at, per * TILE)

        def right_copies():
            return copies(rights, right_refs, right_all, right_sems, 0, 0, wide_cols)

        @pl.when(i == 0)
        def _():
            for c in left_copies(0):
                c.start()
            for c in right_copies():
                c.start()
            for n in range(1, steps):
                for c in left_copies(n):
                    c.start()
            for c in left_copies(0):
                c.wait()
            turned[0] = left_all[:, : per * TILE].T
            for n in range(1, steps):
                for c in left_copies(n):
                    c.wait()
            for c in right_copies():
                c.wait()

        now = lax.rem(i, 2)
        for b in range(0, count_cols, 4):
            n = min(4, count_cols - b)
            sums = jnp.dot(
                turned[now], right_all[:, b * TILE : (b + n) * TILE], preferred_element_type=jnp.float32
            )
            for a in range(per):
                for e in range(n):
                    tile = meta[(first + i * per + a) * count_cols + b + e]
                    found[tile] = sums[a * TILE : (a + 1) * TILE, e * TILE : (e + 1) * TILE] * factor
        for a in range(per if steps > 1 else 0):
            ahead = jnp.minimum(i + 1, steps - 1) * per + a
            turned[1 - now, a * TILE : (a + 1) * TILE, :] = left_all[
                :, pl.ds(pl.multiple_of(ahead * TILE, TILE), TILE)
            ].T

        def out_copies(low, high, begin):
            many = (high - low) // OUT_CHUNK

            def copy(at, size, sem):
                c = pltpu.make_async_copy(found.at[pl.ds(at, size)], out_ref.at[pl.ds(at, size)], sem)
                c.start() if begin else c.wait()

            def chunk(n, c):
                copy(low + n * OUT_CHUNK, OUT_CHUNK, out_sems.at[0])
                return c

            def single(n, c):
                copy(n, 1, out_sems.at[1])
                return c

            lax.fori_loop(0, many, chunk, 0)
            lax.fori_loop(low + many * OUT_CHUNK, high, single, 0)

        def bounds(n):
            row = spots + first + n * per
            return meta[row], meta[row + per]

        out_copies(*bounds(i), True)

        @pl.when(i == steps - 1)
        def _():
            for n in range(steps):
                out_copies(*bounds(n), False)

    operands = [a for a, _, _ in lefts] + [a for a, _, _ in rights]
    aliases = {}
    if before is not None:
        aliases = {1 + len(operands): 0}
        operands.append(before)
    return pl.pallas_call(
        kernel,
        out_shape=jax.ShapeDtypeStruct((kept_tiles, TILE, TILE), jnp.float32),
        grid_spec=pltpu.PrefetchScalarGridSpec(
            num_scalar_prefetch=1,
            grid=(steps,),
            in_specs=[pl.BlockSpec(memory_space=pl.ANY)] * len(operands),
            out_specs=pl.BlockSpec(memory_space=pl.ANY),
            scratch_shapes=[
                pltpu.VMEM((tokens, wide_rows), jnp.bfloat16),
                pltpu.VMEM((tokens, wide_cols), jnp.bfloat16),
                pltpu.VMEM((2, per * TILE, tokens), jnp.bfloat16),
                pltpu.VMEM((kept_tiles + 1, TILE, TILE), jnp.float32),
                pltpu.SemaphoreType.DMA((steps, sum(len(e) for _, _, e in lefts))),
                pltpu.SemaphoreType.DMA((sum(len(e) for _, _, e in rights),)),
                pltpu.SemaphoreType.DMA((2,)),
            ],
        ),
        input_output_aliases=aliases,
        compiler_params=params(),
        cost_estimate=pl.CostEstimate(
            flops=2 * tokens * wide_rows * wide_cols,
            bytes_accessed=tokens * (wide_rows + wide_cols) * 2
            + kept_tiles * TILE * TILE * 4 * count // count_rows,
            transcendentals=0,
        ),
        name="wgrad",
    )(meta, *operands)


def add_received(locals_, received, sums, meta, rows, wide, sends, keep, keep_type):
    span = 1024 if wide % 1024 == 0 else wide
    steps, groups = wide // span, span // GROUP

    def kernel(meta, *refs):
        local_refs, refs = refs[: len(locals_)], refs[len(locals_) :]
        code_refs, refs = refs[: 2 * len(received)], refs[2 * len(received) :]
        send_refs, (keep_ref, held) = refs[: len(sends)], refs[len(sends) :]
        step = pl.program_id(0)

        @pl.when(step == 0)
        def _():
            held[...] = jnp.zeros_like(held)

        for g in range(groups):
            here = slice(g * GROUP, (g + 1) * GROUP)
            there = pl.ds(pl.multiple_of(step * span + g * GROUP, GROUP), GROUP)
            totals = []
            for local, others in sums:
                total = local_refs[local][:, here]
                for n in others:
                    eighths = pick_lane(code_refs[2 * n + 1][...], step * groups + g)
                    total = total + decode(code_refs[2 * n][:, here], eighths)
                totals.append(total)
            keep_ref[:, here] = keep(totals, meta).astype(keep_type)
            for n, send in enumerate(sends):
                codes, eighths = encode(send(totals, meta))
                send_refs[n][:, there] = codes
                held[n] = put_lane(held[n], eighths, step * groups + g)

        @pl.when(step == steps - 1)
        def _():
            for n in range(len(sends)):
                send_refs[n][:, wide:] = pack(held[n])

    in_specs = [pl.BlockSpec((rows, span), lambda s, m, e=e: (m[e], s)) for _, e in locals_]
    operands = [v for v, _ in locals_]
    for codes, entry in received:
        in_specs += [
            pl.BlockSpec((rows, span), lambda s, m, e=entry: (m[e], s)),
            pl.BlockSpec((rows, LANES), lambda s, m, e=entry: (m[e], wide // LANES)),
        ]
        operands += [codes, codes]
    outs = [jax.ShapeDtypeStruct((rows, wide + LANES), jnp.int16)] * len(sends)
    out_specs = [pl.BlockSpec((rows, wide + LANES), lambda s, m: (0, 0))] * len(sends)
    outs.append(jax.ShapeDtypeStruct((rows, wide), keep_type))
    out_specs.append(pl.BlockSpec((rows, span), lambda s, m: (0, s)))
    return pl.pallas_call(
        kernel,
        out_shape=outs,
        grid_spec=pltpu.PrefetchScalarGridSpec(
            num_scalar_prefetch=1,
            grid=(steps,),
            in_specs=in_specs,
            out_specs=out_specs,
            scratch_shapes=[pltpu.VMEM((max(len(sends), 1), rows, LANES), jnp.float32)],
        ),
        compiler_params=params(),
        cost_estimate=pl.CostEstimate(
            flops=8 * rows * wide, bytes_accessed=len(operands) * rows * wide * 3, transcendentals=0
        ),
        name="add_received",
    )(meta, *operands)


def tile_places(tile_rows, tile_cols, count_rows, count_cols):
    kept = tile_rows.shape[0]
    position = tile_rows * count_cols + tile_cols
    short = jnp.arange(kept, dtype=jnp.int32) - kept
    spot = jnp.arange(count_rows * count_cols, dtype=jnp.int32)
    places = jnp.sum(jnp.where(position[None, :] == spot[:, None], short[None, :], 0), axis=1) + kept
    rows = jnp.arange(count_rows, dtype=jnp.int32)
    ends = jnp.sum((tile_rows[None, :] <= rows[:, None]).astype(jnp.int32), axis=1)
    return places, ends


def tables(tile_rows, tile_cols, count_rows, count_cols, extras):
    places, ends = tile_places(tile_rows, tile_cols, count_rows, count_cols)
    return jnp.concatenate([places, jnp.zeros((1,), jnp.int32), ends, extras])


def shards_general(activations, weight_tiles, tile_rows, tile_cols, grad_out):
    tiles = weight_tiles[0, 0]
    count_rows = activations.shape[2] // TILE
    count_cols = grad_out.shape[2] // TILE
    meta = tables(tile_rows[0, 0], tile_cols[0, 0], count_rows, count_cols, jnp.zeros((1,), jnp.int32))
    zero = count_rows * count_cols + 1 + count_rows
    act = lax.all_gather(activations[0], "col", axis=0, tiled=True)
    grad = lax.all_gather(grad_out[0], "row", axis=0, tiled=True)
    tokens = act.shape[0]
    back, weight = strip_matmul([(grad, tokens, None)], meta, (tiles,), count_rows, count_cols, True, 0, tokens, False)
    (partial,) = strip_matmul([(act, tokens, None)], meta, weight, count_rows, count_cols, False, 0, tokens, False)
    output = lax.psum_scatter(partial, "row", scatter_dimension=0, tiled=True).astype(jnp.bfloat16)[None]
    grad_input = lax.psum_scatter(back, "col", scatter_dimension=0, tiled=True).astype(jnp.bfloat16)[None]
    groups = lax.axis_size("depth")
    all_act = lax.all_gather(act, "depth", axis=0, tiled=True)
    all_grad = lax.all_gather(grad, "depth", axis=0, tiled=True)
    grad_tiles = tile_products(
        [(all_act, tokens * groups, [zero])],
        [(all_grad, tokens * groups, [zero])],
        meta,
        tiles.shape[0],
        count_rows,
        count_cols,
        1.0 / math.sqrt(tokens * groups),
        (0, count_rows),
        None,
    )
    return output, grad_input, grad_tiles[None, None]


FIRST_SET, SECOND_SET = (0, 1, 2, 6), (3, 4, 5, 7)


def block_pairs():
    spot = {k: (1, n) for n, k in enumerate(FIRST_SET)} | {k: (0, n) for n, k in enumerate(SECOND_SET)}
    return [(spot[n], spot[n + 4]) for n in range(4)]


def pair_entries(row, col, size, groups):
    y, z0, z1 = col % 2, col // 2 % 2, col // 4
    keep = [p[z1 != row] for p in (block_pairs()[n ^ (col % 4)] for n in range(4))]
    return {
        "dgrad": [1 - y, 3 - y, y, 2 + y],
        "near": [int(z1 != row)],
        "z0": [z0, 1 - z0],
        "mine": [int(z1 == row)],
        "const": [0, 1],
        "left": [g * size + (col ^ k) for g in range(groups) for k in FIRST_SET + SECOND_SET],
        "right": [2 * g + r for g in range(groups) for r in (row, 1 - row)],
        "codes": [n ^ (col % 4) for n in range(4)],
        "second": [1 - k[0] for k in keep],
        "in_first": [k[1] * k[0] for k in keep],
        "in_second": [k[1] * (1 - k[0]) for k in keep],
    }


def swap(value, axis, bit, size):
    return lax.ppermute(value, axis, [(i, i ^ bit) for i in range(size)])


def shards_paired(activations, weight_tiles, tile_rows, tile_cols, grad_out):
    tiles = weight_tiles[0, 0]
    count_rows = activations.shape[2] // TILE
    count_cols = grad_out.shape[2] // TILE
    wide_rows = activations.shape[2]
    size = lax.axis_size("col")
    groups = lax.axis_size("depth")
    row, col = lax.axis_index("row"), lax.axis_index("col")
    block = activations.shape[1]
    half = grad_out.shape[1]
    values = [[sum(pair_entries(r, c, size, groups).values(), []) for c in range(size)] for r in range(2)]
    extras = lax.dynamic_slice(
        jnp.asarray(np.array(values, np.int32)), (row, col, 0), (1, 1, len(values[0][0]))
    ).reshape(-1)
    meta = tables(tile_rows[0, 0], tile_cols[0, 0], count_rows, count_cols, extras)
    at, n = {}, count_rows * count_cols + 1 + count_rows
    for name, entries in pair_entries(0, 0, size, groups).items():
        at[name] = n
        n += len(entries)

    def swap_col(value, bit):
        return swap(value, "col", bit, size)

    def swap_depth(value):
        return swap(value, "depth", 1, 2)

    def swap_row(value):
        return swap(value, "row", 1, 2)

    grad_mine = grad_out[0]
    own = activations[0]
    grad_other = swap_row(grad_mine)
    b2 = swap_col(own, 2)
    b6 = swap_col(own, 6)
    b1 = swap_col(own, 1)
    b3 = swap_col(b1, 2)
    b4 = swap_col(b6, 2)
    b7 = swap_col(b6, 1)
    b5 = swap_col(b7, 2)

    def dgrad(grad, weight):
        blocks = [(grad, block, at["dgrad"] + e) for e in range(4)]
        return strip_matmul(blocks, meta, weight, count_rows, count_cols, True, 2 * block, 2 * block, False)

    def forward(blocks, weight, instead):
        blocks = [(b, block, None) for b in blocks]
        return strip_matmul(blocks, meta, weight, count_rows, count_cols, False, half, half, True, instead)

    codes_mine, kept_mine, weight = dgrad(grad_mine, (tiles,))
    codes_mine = swap_col(codes_mine, 1)
    first_codes, first_kept, first_act = forward([own, b1, b2, b6], weight, None)
    codes_other, kept_other = dgrad(grad_other, weight)
    codes_other = swap_col(codes_other, 1)
    out_codes, second_kept, second_act = forward([b3, b4, b5, b7], weight, (first_codes, at["near"], block_pairs()))
    out_codes = swap_row(out_codes)

    z0, const, mine = at["z0"], at["const"], at["mine"]

    def choose(yes, no):
        return lambda s, m: jnp.where(m[mine] == 1, s[yes], s[no])

    *codes, kept = add_received(
        [(v, z0 + e) for v in (kept_mine, kept_other) for e in (0, 1)],
        [(v, z0 + e) for v in (codes_mine, codes_other) for e in (0, 1)],
        [(n, [n]) for n in range(4)],
        meta,
        block,
        wide_rows,
        [choose(1, 3), choose(2, 0), choose(3, 1)],
        choose(0, 2),
        jnp.float32,
    )
    codes = [swap_col(v, 2 * n + 2) for n, v in enumerate(codes)]

    partner = [swap_depth(v) for v in (first_act, second_act, grad_mine, grad_other)]
    lefts = [
        (v, block, [at["left"] + 4 * n + k for k in range(4)])
        for n, v in enumerate((first_act, second_act, *partner[:2]))
    ]
    rights = [(v, half, [at["right"] + n]) for n, v in enumerate((grad_mine, grad_other, *partner[2:]))]

    def wgrad(part, before):
        return tile_products(
            lefts,
            rights,
            meta,
            tiles.shape[0],
            count_rows,
            count_cols,
            1.0 / math.sqrt(size * block * groups),
            part,
            before,
        )

    grad_tiles = wgrad((0, count_rows), None)
    (grad_input,) = add_received(
        [(kept, const)],
        [(v, const) for v in codes],
        [(0, [0, 1, 2])],
        meta,
        block,
        wide_rows,
        [],
        lambda s, m: s[0],
        jnp.bfloat16,
    )
    output = join_output(first_kept, second_kept, out_codes, meta, at, block)
    return output[None], grad_input[None], grad_tiles[None, None]


def join_output(first, second, codes, meta, at, rows):
    wide = first.shape[1]
    blocks = first.shape[0] // rows

    def kernel(meta, first_ref, second_ref, codes_ref, out_ref):
        use_second = meta[at["second"] + pl.program_id(0)] == 1
        for g in range(wide // GROUP):
            here = slice(g * GROUP, (g + 1) * GROUP)
            local = jnp.where(use_second, second_ref[:, here], first_ref[:, here])
            eighths = pick_lane(codes_ref[:, wide:], g)
            out_ref[:, here] = (local + decode(codes_ref[:, here], eighths)).astype(jnp.bfloat16)

    return pl.pallas_call(
        kernel,
        out_shape=jax.ShapeDtypeStruct((blocks * rows, wide), jnp.bfloat16),
        grid_spec=pltpu.PrefetchScalarGridSpec(
            num_scalar_prefetch=1,
            grid=(blocks,),
            in_specs=[
                pl.BlockSpec((rows, wide), lambda n, m: (m[at["in_first"] + n], 0)),
                pl.BlockSpec((rows, wide), lambda n, m: (m[at["in_second"] + n], 0)),
                pl.BlockSpec((rows, wide + LANES), lambda n, m: (m[at["codes"] + n], 0)),
            ],
            out_specs=pl.BlockSpec((rows, wide), lambda n, m: (n, 0)),
        ),
        compiler_params=params(),
        cost_estimate=pl.CostEstimate(flops=8 * first.size, bytes_accessed=first.size * 8, transcendentals=0),
        name="join_output",
    )(meta, first, second, codes)


def solution(mesh):
    specs = (
        P("depth", "col", "row"),
        P("row", "col", None, None, None),
        P("row", "col", None),
        P("row", "col", None),
        P("depth", "row", "col"),
    )
    paired = mesh.shape["row"] == 2 and mesh.shape["col"] == 8 and mesh.shape["depth"] == 2

    def body(*args):
        return (shards_paired if paired else shards_general)(*args)

    return jax.shard_map(
        body,
        mesh=mesh,
        in_specs=specs,
        out_specs=(specs[4], specs[0], specs[1]),
        check_vma=False,
    )
```

```python
import math

import jax
import jax.numpy as jnp
import numpy as np
from jax import lax
from jax.experimental import pallas as pl
from jax.experimental.pallas import tpu as pltpu
from jax.sharding import PartitionSpec as P


TILE = 128
GROUP = 2 * TILE
LANES = 128
WHOLE = 12582912.0
CHUNK = 32
OUT_CHUNK = 16
LEVELS = 32600.0
SMALL = 1e-30
VMEM_LIMIT = 63 * 1024 * 1024


def params(limit=VMEM_LIMIT):
    return pltpu.CompilerParams(vmem_limit_bytes=limit)


def encode(values):
    top = jnp.maximum(jnp.max(jnp.abs(values), axis=1, keepdims=True), SMALL)
    eighths = jnp.ceil(8.0 * jnp.log2(top * (1.0 / LEVELS)))
    codes = (values * jnp.exp2(eighths * -0.125) + WHOLE) - WHOLE
    return pack(codes), eighths


def decode(codes, eighths):
    return codes.astype(jnp.int32).astype(jnp.float32) * jnp.exp2(eighths * 0.125)


def lane_of(shape):
    return lax.broadcasted_iota(jnp.int32, shape, len(shape) - 1)


def pick_lane(values, lane):
    values = values.astype(jnp.int32).astype(jnp.float32)
    return jnp.sum(jnp.where(lane_of(values.shape) == lane, values, 0.0), axis=1, keepdims=True)


def put_lane(values, column, lane):
    return jnp.where(lane_of(values.shape) == lane, column, values)


def pack(values):
    return values.astype(jnp.int32).astype(jnp.int16)


def strip_matmul(blocks, meta, weight, count_rows, count_cols, along_rows, coded, kept, gathered, swapped=None):
    builds = isinstance(weight, tuple)
    outer_tiles = count_rows if along_rows else count_cols
    width = next(w for w in (GROUP * 4, GROUP * 2, GROUP) if outer_tiles * TILE % w == 0)
    if not along_rows:
        width = min(width, GROUP * 2)
    per = width // TILE
    steps = outer_tiles // per
    inner = (count_cols if along_rows else count_rows) * TILE
    outer = outer_tiles * TILE
    tokens = sum(rows for _, rows, _ in blocks)
    first_kept = tokens - kept
    strip_shape = (width, inner) if along_rows else (inner, width)
    if builds:
        (tiles,) = weight
        kept_tiles = tiles.shape[0]
        chunk = CHUNK if kept_tiles % CHUNK == 0 else kept_tiles
        chunks = kept_tiles // chunk

    def kernel(meta, *refs):
        ins, refs = refs[: len(blocks)], refs[len(blocks) :]
        weight_ref, refs = refs[0], refs[1:]
        if coded:
            codes_ref, refs = refs[0], refs[1:]
        if kept:
            kept_ref, refs = refs[0], refs[1:]
        if gathered:
            gathered_ref, refs = refs[0], refs[1:]
        if builds:
            built_ref, refs = refs[0], refs[1:]
        held, refs = refs[0], refs[1:]
        if coded:
            waiting, refs = refs[0], refs[1:]
        step = pl.program_id(0)

        @pl.when(step == 0)
        def _():
            held[...] = jnp.zeros_like(held)
            if coded:
                waiting[1] = jnp.zeros((coded, width), jnp.float32)

        if builds:
            local, sems = refs

            def chunk_copy(n):
                here = pl.ds(n * chunk, chunk)
                return pltpu.make_async_copy(weight_ref.at[here], local.at[here], sems.at[n])

            @pl.when(step == 0)
            def _():
                for n in range(chunks):
                    chunk_copy(n).start()
                local[kept_tiles] = jnp.zeros((TILE, TILE), jnp.bfloat16)

            base = count_rows * count_cols
            held_chunks = (meta[base + step * per] + (chunk - 1)) // chunk
            needed = jnp.where(step == steps - 1, chunks, (meta[base + step * per + per] + (chunk - 1)) // chunk)
            lax.fori_loop(held_chunks, needed, lambda n, c: (chunk_copy(n).wait(), c)[1], 0)

            for a in range(per):
                for c in range(count_cols):
                    tile = meta[(step * per + a) * count_cols + c]
                    built_ref[a * TILE : (a + 1) * TILE, c * TILE : (c + 1) * TILE] = local[tile]
            strip = built_ref[...]
        else:
            strip = weight_ref[...]
        x = jnp.concatenate([r[...] for r in ins], axis=0) if len(ins) > 1 else ins[0][...]
        if along_rows:
            y = lax.dot_general(x, strip, (((1,), (1,)), ((), ())), preferred_element_type=jnp.float32)
        else:
            y = jnp.dot(x, strip, preferred_element_type=jnp.float32)
        first, last = y[:coded], y[first_kept:]
        if swapped is not None:
            turn = meta[swapped] == 1
            first, last = jnp.where(turn, last, first), jnp.where(turn, first, last)
        if coded:

            def write_codes(values, step):
                for g in range(width // GROUP):
                    codes, eighths = encode(values[:, g * GROUP : (g + 1) * GROUP])
                    here = pl.ds(pl.multiple_of(step * width + g * GROUP, GROUP), GROUP)
                    codes_ref[:, here] = codes
                    held[...] = put_lane(held[...], eighths, step * (width // GROUP) + g)

            write_codes(waiting[1 - lax.rem(step, 2)], jnp.maximum(step - 1, 0))
            waiting[lax.rem(step, 2)] = first

            @pl.when(step == steps - 1)
            def _():
                write_codes(waiting[(steps - 1) % 2], steps - 1)
                codes_ref[:, outer:] = pack(held[...])

        if kept:
            kept_ref[...] = last
        if gathered:

            @pl.when(step == 0)
            def _():
                gathered_ref[...] = x

    def in_spec(rows, entry):
        def place(step, meta):
            return (0 if entry is None else meta[entry], 0)

        return pl.BlockSpec((rows, inner), place, pipeline_mode=pl.Buffered(1))

    outs, out_specs = [], []
    if coded:
        outs.append(jax.ShapeDtypeStruct((coded, outer + LANES), jnp.int16))
        out_specs.append(pl.BlockSpec((coded, outer + LANES), lambda s, m: (0, 0)))
    if kept:
        outs.append(jax.ShapeDtypeStruct((kept, outer), jnp.float32))
        out_specs.append(pl.BlockSpec((kept, width), lambda s, m: (0, s)))
    if gathered:
        outs.append(jax.ShapeDtypeStruct((tokens, inner), jnp.bfloat16))
        out_specs.append(pl.BlockSpec((tokens, inner), lambda s, m: (0, 0)))
    scratch = [pltpu.VMEM((max(coded, 8), LANES), jnp.float32)]
    if coded:
        scratch.append(pltpu.VMEM((2, coded, width), jnp.float32))
    strip_spec = pl.BlockSpec(strip_shape, (lambda s, m: (s, 0)) if along_rows else (lambda s, m: (0, s)))
    if builds:
        outs.append(jax.ShapeDtypeStruct((count_rows * TILE, count_cols * TILE), jnp.bfloat16))
        out_specs.append(strip_spec)
        strip_spec = pl.BlockSpec(memory_space=pl.ANY)
        scratch += [pltpu.VMEM((kept_tiles + 1, TILE, TILE), jnp.bfloat16), pltpu.SemaphoreType.DMA((chunks,))]
    return pl.pallas_call(
        kernel,
        out_shape=outs,
        grid_spec=pltpu.PrefetchScalarGridSpec(
            num_scalar_prefetch=1,
            grid=(steps,),
            in_specs=[in_spec(rows, entry) for _, rows, entry in blocks]
            + [strip_spec],
            out_specs=out_specs,
            scratch_shapes=scratch,
        ),
        compiler_params=params(),
        cost_estimate=pl.CostEstimate(
            flops=2 * tokens * inner * outer,
            bytes_accessed=inner * outer * 2 + tokens * (inner * 2 + outer * 4),
            transcendentals=0,
        ),
        name="dgrad" if along_rows else "forward",
    )(meta, *[a for a, _, _ in blocks], tiles if builds else weight)


def tile_products(lefts, rights, meta, kept_tiles, count_rows, count_cols, factor, part, before):
    tokens = sum(rows * len(entries) for _, rows, entries in lefts)
    first, count = part
    wide_rows, wide_cols = count * TILE, count_cols * TILE
    per = next(p for p in (8, 4, 2, 1) if count % p == 0)
    steps = count // per
    spots = count_rows * count_cols

    def kernel(meta, *refs):
        left_refs, refs = refs[: len(lefts)], refs[len(lefts) :]
        right_refs, refs = refs[: len(rights)], refs[len(rights) :]
        if before is not None:
            refs = refs[1:]
        out_ref, left_all, right_all, turned, found, left_sems, right_sems, out_sems = refs
        i = pl.program_id(0)

        def copies(group, group_refs, whole, sems, from_col, to_col, width):
            n = 0
            for (_, rows, entries), ref in zip(group, group_refs):
                for b, entry in enumerate(entries):
                    to = pl.multiple_of(meta[entry] * rows, rows)
                    yield pltpu.make_async_copy(
                        ref.at[pl.ds(b * rows, rows), pl.ds(from_col, width)],
                        whole.at[pl.ds(to, rows), pl.ds(to_col, width)],
                        sems.at[n],
                    )
                    n += 1

        def left_copies(step):
            at = step * per * TILE
            return copies(lefts, left_refs, left_all, left_sems.at[step], first * TILE + at, at, per * TILE)

        pieces = [(b, min(4, count_cols - b)) for b in range(0, count_cols, 4)]

        def right_copies(p):
            at, width = pieces[p][0] * TILE, pieces[p][1] * TILE
            return copies(rights, right_refs, right_all, right_sems.at[p], at, at, width)

        def wait(group):
            for c in group:
                c.wait()

        def work(opening):
            now = 0 if opening else lax.rem(i, 2)
            for p, (b, n) in enumerate(pieces):
                if opening:
                    wait(right_copies(p))
                sums = jnp.dot(
                    turned[now], right_all[:, b * TILE : (b + n) * TILE], preferred_element_type=jnp.float32
                )
                for a in range(per):
                    for e in range(n):
                        tile = meta[(first + i * per + a) * count_cols + b + e]
                        found[tile] = sums[a * TILE : (a + 1) * TILE, e * TILE : (e + 1) * TILE] * factor
            if opening:
                for n in range(1, steps):
                    wait(left_copies(n))
            for a in range(per if steps > 1 else 0):
                ahead = jnp.minimum(i + 1, steps - 1) * per + a
                turned[1 - now, a * TILE : (a + 1) * TILE, :] = left_all[
                    :, pl.ds(pl.multiple_of(ahead * TILE, TILE), TILE)
                ].T

        @pl.when(i == 0)
        def _():
            for c in left_copies(0):
                c.start()
            for p in range(len(pieces)):
                for c in right_copies(p):
                    c.start()
            for n in range(1, steps):
                for c in left_copies(n):
                    c.start()
            wait(left_copies(0))
            turned[0] = left_all[:, : per * TILE].T
            work(True)

        if steps > 1:

            @pl.when(i > 0)
            def _():
                work(False)

        def out_copies(low, high, begin):
            many = (high - low) // OUT_CHUNK

            def copy(at, size, sem):
                c = pltpu.make_async_copy(found.at[pl.ds(at, size)], out_ref.at[pl.ds(at, size)], sem)
                c.start() if begin else c.wait()

            def chunk(n, c):
                copy(low + n * OUT_CHUNK, OUT_CHUNK, out_sems.at[0])
                return c

            def single(n, c):
                copy(n, 1, out_sems.at[1])
                return c

            lax.fori_loop(0, many, chunk, 0)
            lax.fori_loop(low + many * OUT_CHUNK, high, single, 0)

        def bounds(n):
            row = spots + first + n * per
            return meta[row], meta[row + per]

        out_copies(*bounds(i), True)

        @pl.when(i == steps - 1)
        def _():
            for n in range(steps):
                out_copies(*bounds(n), False)

    operands = [a for a, _, _ in lefts] + [a for a, _, _ in rights]
    aliases = {}
    if before is not None:
        aliases = {1 + len(operands): 0}
        operands.append(before)
    return pl.pallas_call(
        kernel,
        out_shape=jax.ShapeDtypeStruct((kept_tiles, TILE, TILE), jnp.float32),
        grid_spec=pltpu.PrefetchScalarGridSpec(
            num_scalar_prefetch=1,
            grid=(steps,),
            in_specs=[pl.BlockSpec(memory_space=pl.ANY)] * len(operands),
            out_specs=pl.BlockSpec(memory_space=pl.ANY),
            scratch_shapes=[
                pltpu.VMEM((tokens, wide_rows), jnp.bfloat16),
                pltpu.VMEM((tokens, wide_cols), jnp.bfloat16),
                pltpu.VMEM((2, per * TILE, tokens), jnp.bfloat16),
                pltpu.VMEM((kept_tiles + 1, TILE, TILE), jnp.float32),
                pltpu.SemaphoreType.DMA((steps, sum(len(e) for _, _, e in lefts))),
                pltpu.SemaphoreType.DMA((-(-count_cols // 4), sum(len(e) for _, _, e in rights))),
                pltpu.SemaphoreType.DMA((2,)),
            ],
        ),
        input_output_aliases=aliases,
        compiler_params=params(),
        cost_estimate=pl.CostEstimate(
            flops=2 * tokens * wide_rows * wide_cols,
            bytes_accessed=tokens * (wide_rows + wide_cols) * 2
            + kept_tiles * TILE * TILE * 4 * count // count_rows,
            transcendentals=0,
        ),
        name="wgrad",
    )(meta, *operands)


def add_received(locals_, received, sums, meta, rows, wide, sends, keep, keep_type):
    span = wide if len(received) < 4 or wide % 2048 else 2048
    steps, groups = wide // span, span // GROUP

    def kernel(meta, *refs):
        local_refs, refs = refs[: len(locals_)], refs[len(locals_) :]
        code_refs, refs = refs[: 2 * len(received)], refs[2 * len(received) :]
        send_refs, (keep_ref, held) = refs[: len(sends)], refs[len(sends) :]
        step = pl.program_id(0)

        @pl.when(step == 0)
        def _():
            held[...] = jnp.zeros_like(held)

        for g in range(groups):
            here = slice(g * GROUP, (g + 1) * GROUP)
            there = pl.ds(pl.multiple_of(step * span + g * GROUP, GROUP), GROUP)
            totals = []
            for local, others in sums:
                total = local_refs[local][:, here]
                for n in others:
                    eighths = pick_lane(code_refs[2 * n + 1][...], step * groups + g)
                    total = total + decode(code_refs[2 * n][:, here], eighths)
                totals.append(total)
            keep_ref[:, here] = keep(totals, meta).astype(keep_type)
            for n, send in enumerate(sends):
                codes, eighths = encode(send(totals, meta))
                send_refs[n][:, there] = codes
                held[n] = put_lane(held[n], eighths, step * groups + g)

        @pl.when(step == steps - 1)
        def _():
            for n in range(len(sends)):
                send_refs[n][:, wide:] = pack(held[n])

    in_specs = [pl.BlockSpec((rows, span), lambda s, m, e=e: (m[e], s)) for _, e in locals_]
    operands = [v for v, _ in locals_]
    for codes, entry in received:
        in_specs += [
            pl.BlockSpec((rows, span), lambda s, m, e=entry: (m[e], s)),
            pl.BlockSpec((rows, LANES), lambda s, m, e=entry: (m[e], wide // LANES)),
        ]
        operands += [codes, codes]
    outs = [jax.ShapeDtypeStruct((rows, wide + LANES), jnp.int16)] * len(sends)
    out_specs = [pl.BlockSpec((rows, wide + LANES), lambda s, m: (0, 0))] * len(sends)
    outs.append(jax.ShapeDtypeStruct((rows, wide), keep_type))
    out_specs.append(pl.BlockSpec((rows, span), lambda s, m: (0, s)))
    return pl.pallas_call(
        kernel,
        out_shape=outs,
        grid_spec=pltpu.PrefetchScalarGridSpec(
            num_scalar_prefetch=1,
            grid=(steps,),
            in_specs=in_specs,
            out_specs=out_specs,
            scratch_shapes=[pltpu.VMEM((max(len(sends), 1), rows, LANES), jnp.float32)],
        ),
        compiler_params=params(),
        cost_estimate=pl.CostEstimate(
            flops=8 * rows * wide, bytes_accessed=len(operands) * rows * wide * 3, transcendentals=0
        ),
        name="add_received",
    )(meta, *operands)


def tile_places(tile_rows, tile_cols, count_rows, count_cols):
    kept = tile_rows.shape[0]
    position = tile_rows * count_cols + tile_cols
    short = jnp.arange(kept, dtype=jnp.int32) - kept
    spot = jnp.arange(count_rows * count_cols, dtype=jnp.int32)
    places = jnp.sum(jnp.where(position[None, :] == spot[:, None], short[None, :], 0), axis=1) + kept
    rows = jnp.arange(count_rows, dtype=jnp.int32)
    ends = jnp.sum((tile_rows[None, :] <= rows[:, None]).astype(jnp.int32), axis=1)
    return places, ends


def tables(tile_rows, tile_cols, count_rows, count_cols, extras):
    places, ends = tile_places(tile_rows, tile_cols, count_rows, count_cols)
    return jnp.concatenate([places, jnp.zeros((1,), jnp.int32), ends, extras])


def shards_general(activations, weight_tiles, tile_rows, tile_cols, grad_out):
    tiles = weight_tiles[0, 0]
    count_rows = activations.shape[2] // TILE
    count_cols = grad_out.shape[2] // TILE
    meta = tables(tile_rows[0, 0], tile_cols[0, 0], count_rows, count_cols, jnp.zeros((1,), jnp.int32))
    zero = count_rows * count_cols + 1 + count_rows
    act = lax.all_gather(activations[0], "col", axis=0, tiled=True)
    grad = lax.all_gather(grad_out[0], "row", axis=0, tiled=True)
    tokens = act.shape[0]
    back, weight = strip_matmul([(grad, tokens, None)], meta, (tiles,), count_rows, count_cols, True, 0, tokens, False)
    (partial,) = strip_matmul([(act, tokens, None)], meta, weight, count_rows, count_cols, False, 0, tokens, False)
    output = lax.psum_scatter(partial, "row", scatter_dimension=0, tiled=True).astype(jnp.bfloat16)[None]
    grad_input = lax.psum_scatter(back, "col", scatter_dimension=0, tiled=True).astype(jnp.bfloat16)[None]
    groups = lax.axis_size("depth")
    all_act = lax.all_gather(act, "depth", axis=0, tiled=True)
    all_grad = lax.all_gather(grad, "depth", axis=0, tiled=True)
    grad_tiles = tile_products(
        [(all_act, tokens * groups, [zero])],
        [(all_grad, tokens * groups, [zero])],
        meta,
        tiles.shape[0],
        count_rows,
        count_cols,
        1.0 / math.sqrt(tokens * groups),
        (0, count_rows),
        None,
    )
    return output, grad_input, grad_tiles[None, None]


def pair_entries(row, col, size, groups):
    y, z0, z1 = col % 2, col // 2 % 2, col // 4
    return {
        "dgrad": [1 - y, 3 - y, y, 2 + y],
        "far": [int(z1 == row)],
        "z0": [z0, 1 - z0],
        "mine": [int(z1 == row)],
        "const": [0, 1],
        "left": [g * size + (col ^ k) for g in range(groups) for k in range(size)],
        "right": [2 * g + r for g in range(groups) for r in (row, 1 - row)],
        "codes": [n ^ (col % 4) for n in range(4)],
    }


def swap(value, axis, bit, size):
    return lax.ppermute(value, axis, [(i, i ^ bit) for i in range(size)])


def shards_paired(activations, weight_tiles, tile_rows, tile_cols, grad_out):
    tiles = weight_tiles[0, 0]
    count_rows = activations.shape[2] // TILE
    count_cols = grad_out.shape[2] // TILE
    wide_rows = activations.shape[2]
    size = lax.axis_size("col")
    groups = lax.axis_size("depth")
    row, col = lax.axis_index("row"), lax.axis_index("col")
    block = activations.shape[1]
    half = grad_out.shape[1]
    values = [[sum(pair_entries(r, c, size, groups).values(), []) for c in range(size)] for r in range(2)]
    extras = lax.dynamic_slice(
        jnp.asarray(np.array(values, np.int32)), (row, col, 0), (1, 1, len(values[0][0]))
    ).reshape(-1)
    meta = tables(tile_rows[0, 0], tile_cols[0, 0], count_rows, count_cols, extras)
    at, n = {}, count_rows * count_cols + 1 + count_rows
    for name, entries in pair_entries(0, 0, size, groups).items():
        at[name] = n
        n += len(entries)

    def swap_col(value, bit):
        return swap(value, "col", bit, size)

    def swap_depth(value):
        return swap(value, "depth", 1, 2)

    def swap_row(value):
        return swap(value, "row", 1, 2)

    grad_mine = grad_out[0]
    own = activations[0]
    grad_other = swap_row(grad_mine)
    b2 = swap_col(own, 2)
    b6 = swap_col(own, 6)
    b1 = swap_col(own, 1)
    b3 = swap_col(b1, 2)
    b4 = swap_col(b6, 2)
    b7 = swap_col(b6, 1)
    b5 = swap_col(b7, 2)

    def dgrad(grad, weight):
        blocks = [(grad, block, at["dgrad"] + e) for e in range(4)]
        return strip_matmul(blocks, meta, weight, count_rows, count_cols, True, 2 * block, 2 * block, False)

    codes_mine, kept_mine, weight = dgrad(grad_mine, (tiles,))
    codes_mine = swap_col(codes_mine, 1)
    codes_other, kept_other = dgrad(grad_other, weight)
    codes_other = swap_col(codes_other, 1)
    out_codes, out_kept, act = strip_matmul(
        [(b, block, None) for b in (own, b1, b2, b3, b4, b5, b6, b7)],
        meta,
        weight,
        count_rows,
        count_cols,
        False,
        half,
        half,
        True,
        at["far"],
    )
    out_codes = swap_row(out_codes)

    z0, const, mine = at["z0"], at["const"], at["mine"]

    def choose(yes, no):
        return lambda s, m: jnp.where(m[mine] == 1, s[yes], s[no])

    *codes, kept = add_received(
        [(v, z0 + e) for v in (kept_mine, kept_other) for e in (0, 1)],
        [(v, z0 + e) for v in (codes_mine, codes_other) for e in (0, 1)],
        [(n, [n]) for n in range(4)],
        meta,
        block,
        wide_rows,
        [choose(1, 3), choose(2, 0), choose(3, 1)],
        choose(0, 2),
        jnp.float32,
    )
    codes = [swap_col(v, 2 * n + 2) for n, v in enumerate(codes)]

    partner = [swap_depth(v) for v in (act, grad_mine, grad_other)]
    lefts = [(v, block, [at["left"] + size * n + k for k in range(size)]) for n, v in enumerate((act, partner[0]))]
    rights = [(v, half, [at["right"] + n]) for n, v in enumerate((grad_mine, grad_other, *partner[1:]))]

    def wgrad(part, before):
        return tile_products(
            lefts,
            rights,
            meta,
            tiles.shape[0],
            count_rows,
            count_cols,
            1.0 / math.sqrt(size * block * groups),
            part,
            before,
        )

    grad_tiles = wgrad((0, count_rows), None)
    (grad_input,) = add_received(
        [(kept, const)],
        [(v, const) for v in codes],
        [(0, [0, 1, 2])],
        meta,
        block,
        wide_rows,
        [],
        lambda s, m: s[0],
        jnp.bfloat16,
    )
    output = join_output(out_kept, out_codes, meta, at["codes"], block)
    return output[None], grad_input[None], grad_tiles[None, None]


def join_output(local, codes, meta, first, rows):
    wide = local.shape[1]
    blocks = local.shape[0] // rows

    def kernel(meta, local_ref, codes_ref, out_ref):
        for g in range(wide // GROUP):
            here = slice(g * GROUP, (g + 1) * GROUP)
            eighths = pick_lane(codes_ref[:, wide:], g)
            out_ref[:, here] = (local_ref[:, here] + decode(codes_ref[:, here], eighths)).astype(jnp.bfloat16)

    return pl.pallas_call(
        kernel,
        out_shape=jax.ShapeDtypeStruct((blocks * rows, wide), jnp.bfloat16),
        grid_spec=pltpu.PrefetchScalarGridSpec(
            num_scalar_prefetch=1,
            grid=(blocks,),
            in_specs=[
                pl.BlockSpec((rows, wide), lambda n, m: (m[first + n], 0)),
                pl.BlockSpec((rows, wide + LANES), lambda n, m: (m[first + n], 0)),
            ],
            out_specs=pl.BlockSpec((rows, wide), lambda n, m: (n, 0)),
        ),
        compiler_params=params(),
        cost_estimate=pl.CostEstimate(flops=8 * local.size, bytes_accessed=local.size * 8, transcendentals=0),
        name="join_output",
    )(meta, local, codes)


def solution(mesh):
    specs = (
        P("depth", "col", "row"),
        P("row", "col", None, None, None),
        P("row", "col", None),
        P("row", "col", None),
        P("depth", "row", "col"),
    )
    paired = mesh.shape["row"] == 2 and mesh.shape["col"] == 8 and mesh.shape["depth"] == 2

    def body(*args):
        return (shards_paired if paired else shards_general)(*args)

    return jax.shard_map(
        body,
        mesh=mesh,
        in_specs=specs,
        out_specs=(specs[4], specs[0], specs[1]),
        check_vma=False,
    )
```

```python
import math

import jax
import jax.numpy as jnp
import numpy as np
from jax import lax
from jax.experimental import pallas as pl
from jax.experimental.pallas import tpu as pltpu
from jax.sharding import PartitionSpec as P


TILE = 128
GROUP = 2 * TILE
LANES = 128
WHOLE = 12582912.0
CHUNK = 32
OUT_CHUNK = 16
LEVELS = 32600.0
SMALL = 1e-30
VMEM_LIMIT = 67000000
STRIP_LIMIT = 67000000


def params(limit=VMEM_LIMIT):
    return pltpu.CompilerParams(vmem_limit_bytes=limit)


def encode(values):
    top = jnp.maximum(jnp.max(jnp.abs(values), axis=1, keepdims=True), SMALL)
    eighths = jnp.ceil(8.0 * jnp.log2(top * (1.0 / LEVELS)))
    codes = (values * jnp.exp2(eighths * -0.125) + WHOLE) - WHOLE
    return pack(codes), eighths


def decode(codes, scale):
    return codes.astype(jnp.int32).astype(jnp.float32) * scale


def scales_of(last):
    return jnp.exp2(last.astype(jnp.int32).astype(jnp.float32) * 0.125)


def lane_of(shape):
    return lax.broadcasted_iota(jnp.int32, shape, len(shape) - 1)


def column_of(scales, step, steps, groups, g):
    column = scales[:, g : g + 1]
    for n in range(1, steps):
        column = jnp.where(step == n, scales[:, n * groups + g : n * groups + g + 1], column)
    return column


def put_lane(values, column, lane):
    return jnp.where(lane_of(values.shape) == lane, column, values)


def pack(values):
    return values.astype(jnp.int32).astype(jnp.int16)


def strip_matmul(blocks, meta, weight, count_rows, count_cols, along_rows, coded, kept, gathered, swapped=None):
    builds = isinstance(weight, tuple)
    outer_tiles = count_rows if along_rows else count_cols
    width = next(w for w in (GROUP * 4, GROUP * 2, GROUP) if outer_tiles * TILE % w == 0)
    if not along_rows:
        width = min(width, GROUP * 2)
    per = width // TILE
    steps = outer_tiles // per
    inner = (count_cols if along_rows else count_rows) * TILE
    outer = outer_tiles * TILE
    tokens = sum(rows for _, rows, _ in blocks)
    first_kept = tokens - kept
    strip_shape = (width, inner) if along_rows else (inner, width)
    if builds:
        (tiles,) = weight
        kept_tiles = tiles.shape[0]
        chunk = CHUNK if kept_tiles % CHUNK == 0 else kept_tiles
        chunks = kept_tiles // chunk

    def kernel(meta, *refs):
        ins, refs = refs[: len(blocks)], refs[len(blocks) :]
        weight_ref, refs = refs[0], refs[1:]
        if coded:
            codes_ref, refs = refs[0], refs[1:]
        if kept:
            kept_ref, refs = refs[0], refs[1:]
        if gathered:
            gathered_ref, refs = refs[0], refs[1:]
        if builds:
            built_ref, refs = refs[0], refs[1:]
        held, refs = refs[0], refs[1:]
        if coded:
            waiting, refs = refs[0], refs[1:]
        if gathered:
            gathered_sems, refs = refs[0], refs[1:]
        step = pl.program_id(0)

        def gathered_copies():
            for n, ref in enumerate(ins):
                rows = blocks[n][1]
                yield pltpu.make_async_copy(ref, gathered_ref.at[pl.ds(n * rows, rows), :], gathered_sems.at[n])

        if gathered:

            @pl.when(step == 0)
            def _():
                for c in gathered_copies():
                    c.start()

            @pl.when(step == steps - 1)
            def _():
                for c in gathered_copies():
                    c.wait()

        @pl.when(step == 0)
        def _():
            held[...] = jnp.zeros_like(held)
            if coded:
                waiting[1] = jnp.zeros((coded, width), jnp.float32)

        if builds:
            local, sems = refs

            def chunk_copy(n):
                here = pl.ds(n * chunk, chunk)
                return pltpu.make_async_copy(weight_ref.at[here], local.at[here], sems.at[n])

            @pl.when(step == 0)
            def _():
                for n in range(chunks):
                    chunk_copy(n).start()
                local[kept_tiles] = jnp.zeros((TILE, TILE), jnp.bfloat16)

            base = count_rows * count_cols
            held_chunks = (meta[base + step * per] + (chunk - 1)) // chunk
            needed = jnp.where(step == steps - 1, chunks, (meta[base + step * per + per] + (chunk - 1)) // chunk)
            lax.fori_loop(held_chunks, needed, lambda n, c: (chunk_copy(n).wait(), c)[1], 0)

            for a in range(per):
                for c in range(count_cols):
                    tile = meta[(step * per + a) * count_cols + c]
                    built_ref[a * TILE : (a + 1) * TILE, c * TILE : (c + 1) * TILE] = local[tile]
            strip = built_ref[...]
        else:
            strip = weight_ref[...]
        x = jnp.concatenate([r[...] for r in ins], axis=0) if len(ins) > 1 else ins[0][...]
        if along_rows:
            y = lax.dot_general(x, strip, (((1,), (1,)), ((), ())), preferred_element_type=jnp.float32)
        else:
            y = jnp.dot(x, strip, preferred_element_type=jnp.float32)
        first, last = y[:coded], y[first_kept:]
        if swapped is not None:
            turn = meta[swapped] == 1
            first, last = jnp.where(turn, last, first), jnp.where(turn, first, last)
        if coded:

            def write_codes(values, step):
                for g in range(width // GROUP):
                    codes, eighths = encode(values[:, g * GROUP : (g + 1) * GROUP])
                    here = pl.ds(pl.multiple_of(step * width + g * GROUP, GROUP), GROUP)
                    codes_ref[:, here] = codes
                    held[...] = put_lane(held[...], eighths, step * (width // GROUP) + g)

            write_codes(waiting[1 - lax.rem(step, 2)], jnp.maximum(step - 1, 0))
            waiting[lax.rem(step, 2)] = first

            @pl.when(step == steps - 1)
            def _():
                write_codes(waiting[(steps - 1) % 2], steps - 1)
                codes_ref[:, outer:] = pack(held[...])

        if kept:
            kept_ref[...] = last

    def in_spec(rows, entry):
        def place(step, meta):
            return (0 if entry is None else meta[entry], 0)

        return pl.BlockSpec((rows, inner), place, pipeline_mode=pl.Buffered(1))

    outs, out_specs = [], []
    if coded:
        outs.append(jax.ShapeDtypeStruct((coded, outer + LANES), jnp.int16))
        out_specs.append(pl.BlockSpec((coded, outer + LANES), lambda s, m: (0, 0)))
    if kept:
        outs.append(jax.ShapeDtypeStruct((kept, outer), jnp.float32))
        out_specs.append(pl.BlockSpec((kept, width), lambda s, m: (0, s)))
    if gathered:
        outs.append(jax.ShapeDtypeStruct((tokens, inner), jnp.bfloat16))
        out_specs.append(pl.BlockSpec(memory_space=pl.ANY))
    scratch = [pltpu.VMEM((max(coded, 8), LANES), jnp.float32)]
    if coded:
        scratch.append(pltpu.VMEM((2, coded, width), jnp.float32))
    if gathered:
        scratch.append(pltpu.SemaphoreType.DMA((len(blocks),)))
    strip_spec = pl.BlockSpec(strip_shape, (lambda s, m: (s, 0)) if along_rows else (lambda s, m: (0, s)))
    if builds:
        outs.append(jax.ShapeDtypeStruct((count_rows * TILE, count_cols * TILE), jnp.bfloat16))
        out_specs.append(strip_spec)
        strip_spec = pl.BlockSpec(memory_space=pl.ANY)
        scratch += [pltpu.VMEM((kept_tiles + 1, TILE, TILE), jnp.bfloat16), pltpu.SemaphoreType.DMA((chunks,))]
    return pl.pallas_call(
        kernel,
        out_shape=outs,
        grid_spec=pltpu.PrefetchScalarGridSpec(
            num_scalar_prefetch=1,
            grid=(steps,),
            in_specs=[in_spec(rows, entry) for _, rows, entry in blocks]
            + [strip_spec],
            out_specs=out_specs,
            scratch_shapes=scratch,
        ),
        compiler_params=params(STRIP_LIMIT),
        cost_estimate=pl.CostEstimate(
            flops=2 * tokens * inner * outer,
            bytes_accessed=inner * outer * 2 + tokens * (inner * 2 + outer * 4),
            transcendentals=0,
        ),
        name="dgrad" if along_rows else "forward",
    )(meta, *[a for a, _, _ in blocks], tiles if builds else weight)


def tile_products(lefts, rights, meta, kept_tiles, count_rows, count_cols, factor, part, before):
    tokens = sum(rows * len(entries) for _, rows, entries in lefts)
    first, count = part
    wide_rows, wide_cols = count * TILE, count_cols * TILE
    per = next(p for p in (8, 4, 2, 1) if count % p == 0)
    steps = count // per
    spots = count_rows * count_cols

    def kernel(meta, *refs):
        left_refs, refs = refs[: len(lefts)], refs[len(lefts) :]
        right_refs, refs = refs[: len(rights)], refs[len(rights) :]
        if before is not None:
            refs = refs[1:]
        out_ref, left_all, right_all, turned, found, left_sems, right_sems, out_sems = refs
        i = pl.program_id(0)

        def copies(group, group_refs, whole, sems, from_col, to_col, width):
            n = 0
            for (_, rows, entries), ref in zip(group, group_refs):
                for b, entry in enumerate(entries):
                    to = pl.multiple_of(meta[entry] * rows, rows)
                    yield pltpu.make_async_copy(
                        ref.at[pl.ds(b * rows, rows), pl.ds(from_col, width)],
                        whole.at[pl.ds(to, rows), pl.ds(to_col, width)],
                        sems.at[n],
                    )
                    n += 1

        def left_copies(step):
            at = step * per * TILE
            return copies(lefts, left_refs, left_all, left_sems.at[step], first * TILE + at, at, per * TILE)

        pieces = [(b, min(4, count_cols - b)) for b in range(0, count_cols, 4)]

        def right_copies(p):
            at, width = pieces[p][0] * TILE, pieces[p][1] * TILE
            return copies(rights, right_refs, right_all, right_sems.at[p], at, at, width)

        def wait(group):
            for c in group:
                c.wait()

        def work(opening):
            now = 0 if opening else lax.rem(i, 2)
            for p, (b, n) in enumerate(pieces):
                if opening:
                    wait(right_copies(p))
                sums = jnp.dot(
                    turned[now], right_all[:, b * TILE : (b + n) * TILE], preferred_element_type=jnp.float32
                )
                for a in range(per):
                    for e in range(n):
                        tile = meta[(first + i * per + a) * count_cols + b + e]
                        found[tile] = sums[a * TILE : (a + 1) * TILE, e * TILE : (e + 1) * TILE] * factor
            if opening:
                for n in range(1, steps):
                    wait(left_copies(n))
            for a in range(per if steps > 1 else 0):
                ahead = jnp.minimum(i + 1, steps - 1) * per + a
                turned[1 - now, a * TILE : (a + 1) * TILE, :] = left_all[
                    :, pl.ds(pl.multiple_of(ahead * TILE, TILE), TILE)
                ].T

        @pl.when(i == 0)
        def _():
            for c in left_copies(0):
                c.start()
            for p in range(len(pieces)):
                for c in right_copies(p):
                    c.start()
            for n in range(1, steps):
                for c in left_copies(n):
                    c.start()
            wait(left_copies(0))
            turned[0] = left_all[:, : per * TILE].T
            work(True)

        if steps > 1:

            @pl.when(i > 0)
            def _():
                work(False)

        def out_copies(low, high, begin):
            many = (high - low) // OUT_CHUNK

            def copy(at, size, sem):
                c = pltpu.make_async_copy(found.at[pl.ds(at, size)], out_ref.at[pl.ds(at, size)], sem)
                c.start() if begin else c.wait()

            def chunk(n, c):
                copy(low + n * OUT_CHUNK, OUT_CHUNK, out_sems.at[0])
                return c

            def single(n, c):
                copy(n, 1, out_sems.at[1])
                return c

            lax.fori_loop(0, many, chunk, 0)
            lax.fori_loop(low + many * OUT_CHUNK, high, single, 0)

        def bounds(n):
            row = spots + first + n * per
            return meta[row], meta[row + per]

        out_copies(*bounds(i), True)

        @pl.when(i == steps - 1)
        def _():
            for n in range(steps):
                out_copies(*bounds(n), False)

    operands = [a for a, _, _ in lefts] + [a for a, _, _ in rights]
    aliases = {}
    if before is not None:
        aliases = {1 + len(operands): 0}
        operands.append(before)
    return pl.pallas_call(
        kernel,
        out_shape=jax.ShapeDtypeStruct((kept_tiles, TILE, TILE), jnp.float32),
        grid_spec=pltpu.PrefetchScalarGridSpec(
            num_scalar_prefetch=1,
            grid=(steps,),
            in_specs=[pl.BlockSpec(memory_space=pl.ANY)] * len(operands),
            out_specs=pl.BlockSpec(memory_space=pl.ANY),
            scratch_shapes=[
                pltpu.VMEM((tokens, wide_rows), jnp.bfloat16),
                pltpu.VMEM((tokens, wide_cols), jnp.bfloat16),
                pltpu.VMEM((2, per * TILE, tokens), jnp.bfloat16),
                pltpu.VMEM((kept_tiles + 1, TILE, TILE), jnp.float32),
                pltpu.SemaphoreType.DMA((steps, sum(len(e) for _, _, e in lefts))),
                pltpu.SemaphoreType.DMA((-(-count_cols // 4), sum(len(e) for _, _, e in rights))),
                pltpu.SemaphoreType.DMA((2,)),
            ],
        ),
        input_output_aliases=aliases,
        compiler_params=params(),
        cost_estimate=pl.CostEstimate(
            flops=2 * tokens * wide_rows * wide_cols,
            bytes_accessed=tokens * (wide_rows + wide_cols) * 2
            + kept_tiles * TILE * TILE * 4 * count // count_rows,
            transcendentals=0,
        ),
        name="wgrad",
    )(meta, *operands)


def add_received(locals_, received, sums, meta, rows, wide, sends, keep, keep_type):
    span = wide if len(received) < 4 or wide % 2048 else 2048
    steps, groups = wide // span, span // GROUP

    def kernel(meta, *refs):
        local_refs, refs = refs[: len(locals_)], refs[len(locals_) :]
        code_refs, refs = refs[: 2 * len(received)], refs[2 * len(received) :]
        send_refs, (keep_ref, held) = refs[: len(sends)], refs[len(sends) :]
        step = pl.program_id(0)

        @pl.when(step == 0)
        def _():
            held[...] = jnp.zeros_like(held)

        scales = [scales_of(code_refs[2 * n + 1][...]) for n in range(len(received))]
        marks = [held[n] for n in range(len(sends))]
        for g in range(groups):
            here = slice(g * GROUP, (g + 1) * GROUP)
            there = pl.ds(pl.multiple_of(step * span + g * GROUP, GROUP), GROUP)
            totals = []
            for local, others in sums:
                total = local_refs[local][:, here]
                for n in others:
                    scale = column_of(scales[n], step, steps, groups, g)
                    total = total + decode(code_refs[2 * n][:, here], scale)
                totals.append(total)
            keep_ref[:, here] = keep(totals, meta).astype(keep_type)
            for n, send in enumerate(sends):
                codes, eighths = encode(send(totals, meta))
                send_refs[n][:, there] = codes
                marks[n] = put_lane(marks[n], eighths, step * groups + g)
        for n, mark in enumerate(marks):
            held[n] = mark

        @pl.when(step == steps - 1)
        def _():
            for n in range(len(sends)):
                send_refs[n][:, wide:] = pack(held[n])

    in_specs = [pl.BlockSpec((rows, span), lambda s, m, e=e: (m[e], s)) for _, e in locals_]
    operands = [v for v, _ in locals_]
    for codes, entry in received:
        in_specs += [
            pl.BlockSpec((rows, span), lambda s, m, e=entry: (m[e], s)),
            pl.BlockSpec((rows, LANES), lambda s, m, e=entry: (m[e], wide // LANES)),
        ]
        operands += [codes, codes]
    outs = [jax.ShapeDtypeStruct((rows, wide + LANES), jnp.int16)] * len(sends)
    out_specs = [pl.BlockSpec((rows, wide + LANES), lambda s, m: (0, 0))] * len(sends)
    outs.append(jax.ShapeDtypeStruct((rows, wide), keep_type))
    out_specs.append(pl.BlockSpec((rows, span), lambda s, m: (0, s)))
    return pl.pallas_call(
        kernel,
        out_shape=outs,
        grid_spec=pltpu.PrefetchScalarGridSpec(
            num_scalar_prefetch=1,
            grid=(steps,),
            in_specs=in_specs,
            out_specs=out_specs,
            scratch_shapes=[pltpu.VMEM((max(len(sends), 1), rows, LANES), jnp.float32)],
        ),
        compiler_params=params(),
        cost_estimate=pl.CostEstimate(
            flops=8 * rows * wide, bytes_accessed=len(operands) * rows * wide * 3, transcendentals=0
        ),
        name="add_received",
    )(meta, *operands)


def tile_places(tile_rows, tile_cols, count_rows, count_cols):
    kept = tile_rows.shape[0]
    position = tile_rows * count_cols + tile_cols
    short = jnp.arange(kept, dtype=jnp.int32) - kept
    spot = jnp.arange(count_rows * count_cols, dtype=jnp.int32)
    places = jnp.sum(jnp.where(position[None, :] == spot[:, None], short[None, :], 0), axis=1) + kept
    rows = jnp.arange(count_rows, dtype=jnp.int32)
    ends = jnp.sum((tile_rows[None, :] <= rows[:, None]).astype(jnp.int32), axis=1)
    return places, ends


def tables(tile_rows, tile_cols, count_rows, count_cols, extras):
    places, ends = tile_places(tile_rows, tile_cols, count_rows, count_cols)
    return jnp.concatenate([places, jnp.zeros((1,), jnp.int32), ends, extras])


def shards_general(activations, weight_tiles, tile_rows, tile_cols, grad_out):
    tiles = weight_tiles[0, 0]
    count_rows = activations.shape[2] // TILE
    count_cols = grad_out.shape[2] // TILE
    meta = tables(tile_rows[0, 0], tile_cols[0, 0], count_rows, count_cols, jnp.zeros((1,), jnp.int32))
    zero = count_rows * count_cols + 1 + count_rows
    act = lax.all_gather(activations[0], "col", axis=0, tiled=True)
    grad = lax.all_gather(grad_out[0], "row", axis=0, tiled=True)
    tokens = act.shape[0]
    back, weight = strip_matmul([(grad, tokens, None)], meta, (tiles,), count_rows, count_cols, True, 0, tokens, False)
    (partial,) = strip_matmul([(act, tokens, None)], meta, weight, count_rows, count_cols, False, 0, tokens, False)
    output = lax.psum_scatter(partial, "row", scatter_dimension=0, tiled=True).astype(jnp.bfloat16)[None]
    grad_input = lax.psum_scatter(back, "col", scatter_dimension=0, tiled=True).astype(jnp.bfloat16)[None]
    groups = lax.axis_size("depth")
    all_act = lax.all_gather(act, "depth", axis=0, tiled=True)
    all_grad = lax.all_gather(grad, "depth", axis=0, tiled=True)
    grad_tiles = tile_products(
        [(all_act, tokens * groups, [zero])],
        [(all_grad, tokens * groups, [zero])],
        meta,
        tiles.shape[0],
        count_rows,
        count_cols,
        1.0 / math.sqrt(tokens * groups),
        (0, count_rows),
        None,
    )
    return output, grad_input, grad_tiles[None, None]


def pair_entries(row, col, size, groups):
    y, z0, z1 = col % 2, col // 2 % 2, col // 4
    return {
        "dgrad": [1 - y, 3 - y, y, 2 + y],
        "far": [int(z1 == row)],
        "z0": [z0, 1 - z0],
        "mine": [int(z1 == row)],
        "const": [0, 1],
        "left": [g * size + (col ^ k) for g in range(groups) for k in range(size)],
        "right": [2 * g + r for g in range(groups) for r in (row, 1 - row)],
        "codes": [n ^ (col % 4) for n in range(4)],
    }


def swap(value, axis, bit, size):
    return lax.ppermute(value, axis, [(i, i ^ bit) for i in range(size)])


def shards_paired(activations, weight_tiles, tile_rows, tile_cols, grad_out):
    tiles = weight_tiles[0, 0]
    count_rows = activations.shape[2] // TILE
    count_cols = grad_out.shape[2] // TILE
    wide_rows = activations.shape[2]
    size = lax.axis_size("col")
    groups = lax.axis_size("depth")
    row, col = lax.axis_index("row"), lax.axis_index("col")
    block = activations.shape[1]
    half = grad_out.shape[1]
    values = [[sum(pair_entries(r, c, size, groups).values(), []) for c in range(size)] for r in range(2)]
    extras = lax.dynamic_slice(
        jnp.asarray(np.array(values, np.int32)), (row, col, 0), (1, 1, len(values[0][0]))
    ).reshape(-1)
    meta = tables(tile_rows[0, 0], tile_cols[0, 0], count_rows, count_cols, extras)
    at, n = {}, count_rows * count_cols + 1 + count_rows
    for name, entries in pair_entries(0, 0, size, groups).items():
        at[name] = n
        n += len(entries)

    def swap_col(value, bit):
        return swap(value, "col", bit, size)

    def swap_depth(value):
        return swap(value, "depth", 1, 2)

    def swap_row(value):
        return swap(value, "row", 1, 2)

    grad_mine = grad_out[0]
    own = activations[0]
    grad_other = swap_row(grad_mine)
    b2 = swap_col(own, 2)
    b6 = swap_col(own, 6)
    b1 = swap_col(own, 1)
    b3 = swap_col(b1, 2)
    b4 = swap_col(b6, 2)
    b7 = swap_col(b6, 1)
    b5 = swap_col(b7, 2)

    def dgrad(grad, weight):
        blocks = [(grad, block, at["dgrad"] + e) for e in range(4)]
        return strip_matmul(blocks, meta, weight, count_rows, count_cols, True, 2 * block, 2 * block, False)

    codes_mine, kept_mine, weight = dgrad(grad_mine, (tiles,))
    codes_mine = swap_col(codes_mine, 1)
    codes_other, kept_other = dgrad(grad_other, weight)
    codes_other = swap_col(codes_other, 1)
    out_codes, out_kept, act = strip_matmul(
        [(b, block, None) for b in (own, b1, b2, b3, b4, b5, b6, b7)],
        meta,
        weight,
        count_rows,
        count_cols,
        False,
        half,
        half,
        True,
        at["far"],
    )
    out_codes = swap_row(out_codes)

    z0, const, mine = at["z0"], at["const"], at["mine"]

    def choose(yes, no):
        return lambda s, m: jnp.where(m[mine] == 1, s[yes], s[no])

    *codes, kept = add_received(
        [(v, z0 + e) for v in (kept_mine, kept_other) for e in (0, 1)],
        [(v, z0 + e) for v in (codes_mine, codes_other) for e in (0, 1)],
        [(n, [n]) for n in range(4)],
        meta,
        block,
        wide_rows,
        [choose(1, 3), choose(2, 0), choose(3, 1)],
        choose(0, 2),
        jnp.float32,
    )
    codes = [swap_col(v, 2 * n + 2) for n, v in enumerate(codes)]

    partner = [swap_depth(v) for v in (act, grad_mine, grad_other)]
    lefts = [(v, block, [at["left"] + size * n + k for k in range(size)]) for n, v in enumerate((act, partner[0]))]
    rights = [(v, half, [at["right"] + n]) for n, v in enumerate((grad_mine, grad_other, *partner[1:]))]

    def wgrad(part, before):
        return tile_products(
            lefts,
            rights,
            meta,
            tiles.shape[0],
            count_rows,
            count_cols,
            1.0 / math.sqrt(size * block * groups),
            part,
            before,
        )

    grad_tiles = wgrad((0, count_rows), None)
    (grad_input,) = add_received(
        [(kept, const)],
        [(v, const) for v in codes],
        [(0, [0, 1, 2])],
        meta,
        block,
        wide_rows,
        [],
        lambda s, m: s[0],
        jnp.bfloat16,
    )
    output = join_output(out_kept, out_codes, meta, at["codes"], block)
    return output[None], grad_input[None], grad_tiles[None, None]


def join_output(local, codes, meta, first, rows):
    wide = local.shape[1]
    blocks = local.shape[0] // rows

    def kernel(meta, local_ref, codes_ref, out_ref):
        scales = scales_of(codes_ref[:, wide:])
        for g in range(wide // GROUP):
            here = slice(g * GROUP, (g + 1) * GROUP)
            total = local_ref[:, here] + decode(codes_ref[:, here], scales[:, g : g + 1])
            out_ref[:, here] = total.astype(jnp.bfloat16)

    return pl.pallas_call(
        kernel,
        out_shape=jax.ShapeDtypeStruct((blocks * rows, wide), jnp.bfloat16),
        grid_spec=pltpu.PrefetchScalarGridSpec(
            num_scalar_prefetch=1,
            grid=(blocks,),
            in_specs=[
                pl.BlockSpec((rows, wide), lambda n, m: (m[first + n], 0)),
                pl.BlockSpec((rows, wide + LANES), lambda n, m: (m[first + n], 0)),
            ],
            out_specs=pl.BlockSpec((rows, wide), lambda n, m: (n, 0)),
        ),
        compiler_params=params(),
        cost_estimate=pl.CostEstimate(flops=8 * local.size, bytes_accessed=local.size * 8, transcendentals=0),
        name="join_output",
    )(meta, local, codes)


def solution(mesh):
    specs = (
        P("depth", "col", "row"),
        P("row", "col", None, None, None),
        P("row", "col", None),
        P("row", "col", None),
        P("depth", "row", "col"),
    )
    paired = mesh.shape["row"] == 2 and mesh.shape["col"] == 8 and mesh.shape["depth"] == 2

    def body(*args):
        return (shards_paired if paired else shards_general)(*args)

    return jax.shard_map(
        body,
        mesh=mesh,
        in_specs=specs,
        out_specs=(specs[4], specs[0], specs[1]),
        check_vma=False,
    )
```
